32 devices in a mesh: rep: 4 (over x, core), dp: 2 (over y), ctx: 4 (over z).
Axes of the slice: x: 2, y: 2, z: 4, core: 2. Of those that a mesh axis runs over, the one named last changes fastest.
Arguments:
- hidden_in: bfloat16 [16, 1024, 1600], P(('rep', 'dp'), 'ctx'), may hold values from -6 to 6
- piece_starts: int32 [16, 2], P(('rep', 'dp')), may hold values from 0 to 768, as said below
- grad_out: bfloat16 [16, 1024, 1600], P(('rep', 'dp'), 'ctx'), may hold values from -6 to 6
- attn_gain: bfloat16 [1600], P(('dp', 'ctx')), may hold values from 0.099609375 to 1.8984375
- attn_shift: bfloat16 [1600], P(('dp', 'ctx')), may hold values from -2 to 2
- qkv_weight: bfloat16 [1600, 4800], P(('dp', 'ctx')), may hold values from -0.15625 to 0.15625
- qv_bias: bfloat16 [3200], P(('dp', 'ctx')), may hold values from -2 to 2
- out_weight: bfloat16 [1600, 1600], P(('dp', 'ctx')), may hold values from -0.625 to 0.625
- out_bias: bfloat16 [1600], P(('dp', 'ctx')), may hold values from -2 to 2
- mlp_gain: bfloat16 [1600], P(('dp', 'ctx')), may hold values from 0.099609375 to 1.8984375
- mlp_shift: bfloat16 [1600], P(('dp', 'ctx')), may hold values from -2 to 2
- fc_weight: bfloat16 [1600, 6400], P(('dp', 'ctx')), may hold values from -0.15625 to 0.15625
- fc_bias: bfloat16 [6400], P(('dp', 'ctx')), may hold values from -2 to 2
- proj_weight: bfloat16 [6400, 1600], P(('dp', 'ctx')), may hold values from -0.078125 to 0.078125
- proj_bias: bfloat16 [1600], P(('dp', 'ctx')), may hold values from -2 to 2
Outputs:
- block_out: bfloat16 [16, 1024, 1600], P(('rep', 'dp'), 'ctx')
- grad_input: float32 [16, 1024, 1600], P(('rep', 'dp'), 'ctx')
- grad_attn_gain: float32 [1600], P(('dp', 'ctx'))
- grad_attn_shift: float32 [1600], P(('dp', 'ctx'))
- grad_qkv_weight: float32 [1600, 4800], P(('dp', 'ctx'))
- grad_qv_bias: float32 [3200], P(('dp', 'ctx'))
- grad_out_weight: float32 [1600, 1600], P(('dp', 'ctx'))
- grad_out_bias: float32 [1600], P(('dp', 'ctx'))
- grad_mlp_gain: float32 [1600], P(('dp', 'ctx'))
- grad_mlp_shift: float32 [1600], P(('dp', 'ctx'))
- grad_fc_weight: float32 [1600, 6400], P(('dp', 'ctx'))
- grad_fc_bias: float32 [6400], P(('dp', 'ctx'))
- grad_proj_weight: float32 [6400, 1600], P(('dp', 'ctx'))
- grad_proj_bias: float32 [1600], P(('dp', 'ctx'))
The draws below stay inside these ranges and needn't reach their ends.
Inputs may be any that keep to these rules, and one draw needn't show every extreme that they name: `piece_starts`: each entry is the first position of a bidirectional piece of its sequence, a multiple of 128; pieces of one sequence may intersect.
All inputs are finite; a program needn't handle non-finite values.
Results may differ from the reference program's by a relative error of at most 0.017.
Values may be sent and summed in bfloat16 or wider, within the bound.
No kernel may reach another device: no remote copies, remote signals or barrier semaphores. Data moves between devices by JAX's collectives and lax.ppermute only.
A program may use at most 576 MiB of HBM per device.

```python
import jax
import jax.numpy as jnp
from jax import lax

D = 1600
HEADS = 25
HD = 64
FF = 6400
SEQ = 1024
PIECE = 256
PIECES = 2
SEQS = 16


def draw_piece_starts(key, part):
    slot_count = (SEQ - PIECE) // (PIECE // 2) + 1
    chosen = jax.random.randint(key, (SEQS, PIECES), 0, slot_count)
    first_seq = jax.random.randint(jax.random.fold_in(key, 1), (), 0, SEQS)
    second_seq = jax.random.randint(jax.random.fold_in(key, 2), (), 0, SEQS)
    chosen = chosen.at[first_seq, 0].set(0)
    chosen = chosen.at[second_seq, PIECES - 1].set(slot_count - 1)
    return (chosen * (PIECE // 2)).astype(jnp.int32)


def levels(own_key, shape, split, low, high):
    def one(dim, blocks):
        steps = jax.random.uniform(jax.random.fold_in(jax.random.fold_in(own_key, 6), dim), (blocks,), jnp.float32, low / len(split), high / len(split))
        return jnp.repeat(jnp.exp(steps), shape[dim] // blocks).reshape((-1,) + (1,) * (len(shape) - dim - 1))

    level = one(*split[0])
    for cut in split[1:]:
        level = level * one(*cut)
    return level


def scatter_about(rng, shape, scale, limit, split=(), kind=jnp.bfloat16):
    drawn = jax.random.normal(rng, shape, jnp.float32) * scale
    if len(split) > 0:
        drawn = levels(rng, shape, split, -0.22, 0.18) * drawn
    return jnp.clip(drawn, min=-limit, max=limit).astype(kind)


def setup_inputs(seed: int = 0) -> dict:
    key_list = jax.random.split(jax.random.key(seed), 16)
    return {
        "hidden_in": scatter_about(key_list[0], (SEQS, SEQ, D), 1.0, 6.0, ((0, 8), (1, 4))),
        "piece_starts": draw_piece_starts(jax.random.fold_in(key_list[15], 71), 0),
        "grad_out": scatter_about(key_list[2], (SEQS, SEQ, D), 1.0, 6.0, ((0, 8), (1, 4))),
        "attn_gain": jnp.clip(1.0 + 0.18 * jax.random.normal(key_list[3], (D,), jnp.float32), 0.099609375, 1.8984375).astype(jnp.bfloat16),
        "attn_shift": scatter_about(key_list[4], (D,), 0.3, 2.0, ((0, 8),)),
        "qkv_weight": scatter_about(key_list[5], (D, 3 * D), D ** -0.5, 0.15625, ((0, 8),)),
        "qv_bias": scatter_about(key_list[6], (2 * D,), 0.3, 2.0, ((0, 8),)),
        "out_weight": scatter_about(key_list[7], (D, D), (D // 16) ** -0.5, 0.625, ((0, 8),)),
        "out_bias": scatter_about(key_list[8], (D,), 0.3, 2.0, ((0, 8),)),
        "mlp_gain": jnp.clip(1.0 + 0.18 * jax.random.normal(key_list[9], (D,), jnp.float32), 0.099609375, 1.8984375).astype(jnp.bfloat16),
        "mlp_shift": scatter_about(key_list[10], (D,), 0.3, 2.0, ((0, 8),)),
        "fc_weight": scatter_about(key_list[11], (D, FF), D ** -0.5, 0.15625, ((0, 8),)),
        "fc_bias": scatter_about(key_list[12], (FF,), 0.3, 2.0, ((0, 8),)),
        "proj_weight": scatter_about(key_list[13], (FF, D), FF ** -0.5, 0.078125, ((0, 8),)),
        "proj_bias": scatter_about(key_list[14], (D,), 0.3, 2.0, ((0, 8),)),
    }


@jax.custom_vjp
def low(v):
    return lax.optimization_barrier(v.astype(jnp.bfloat16)).astype(jnp.float32)

@jax.custom_vjp
def low_back(v):
    return v

def low_keep(v):
    return (low(v), None)

def low_pass(kept, grad):
    return (grad,)

def back_keep(v):
    return (v, None)

def back_low(kept, grad):
    return (low(grad),)
low.defvjp(low_keep, low_pass)
low_back.defvjp(back_keep, back_low)
EPSILON = 1e-05
HIGHEST = lax.Precision.HIGHEST
MASKED = -1000000000.0
gelu_coeff = 0.7978845608028654
gelu_cubic = 0.044715

def matmul(left, right):
    return jnp.dot(left, right, precision=HIGHEST, preferred_element_type=jnp.float32)

def layer_norm(values, gain, shift):
    center = values - lax.optimization_barrier(jnp.mean(values, axis=-1, keepdims=True))
    variance = lax.optimization_barrier(jnp.mean(center * center, axis=-1, keepdims=True))
    return center * lax.rsqrt(variance + EPSILON) * gain + shift

def gelu_tanh(values):
    return 0.5 * values * (1.0 + jnp.tanh(gelu_coeff * (values + gelu_cubic * values * values * values)))

def attend(query, keys, values, starts):
    block_rows = min(512, SEQ)
    key_pos = jnp.arange(SEQ, dtype=jnp.int32)
    key_in = ((key_pos[:, None] >= starts[None, :]) & (key_pos[:, None] < starts[None, :] + PIECE)).astype(jnp.float32)
    keys_heads = keys.reshape(SEQ, HEADS, HD)
    values_heads = values.reshape(SEQ, HEADS, HD)

    def one_block(items):
        query_block, first_row = items
        row_pos = first_row + jnp.arange(block_rows, dtype=jnp.int32)
        row_in = ((row_pos[:, None] >= starts[None, :]) & (row_pos[:, None] < starts[None, :] + PIECE)).astype(jnp.float32)
        shared = matmul(row_in, key_in.T) > 0.5
        allowed = (key_pos[None, :] <= row_pos[:, None]) | shared
        scores = jnp.einsum('thd,shd->hts', query_block.reshape(block_rows, HEADS, HD), keys_heads, precision=HIGHEST) * HD ** (-0.5)
        scores = low_back(jnp.where(allowed[None], scores, MASKED))
        top_score = lax.optimization_barrier(jnp.max(scores, axis=-1, keepdims=True))
        expo = jnp.exp(scores - top_score)
        probs = low(expo / lax.optimization_barrier(jnp.sum(expo, axis=-1, keepdims=True)))
        mixed = jnp.einsum('hts,shd->thd', probs, values_heads, precision=HIGHEST)
        return mixed.reshape(block_rows, D)
    blocks = query.reshape(SEQ // block_rows, block_rows, D)
    firsts = (jnp.arange(SEQ // block_rows, dtype=jnp.int32) * block_rows).astype(jnp.int32)
    result = lax.map(jax.checkpoint(one_block), (blocks, firsts))
    return result.reshape(SEQ, D)

def block_forward(params, seq_in, starts):
    attn_gain, attn_shift, qkv_weight, qv_bias, out_weight, out_bias, mlp_gain, mlp_shift, fc_weight, fc_bias, proj_weight, proj_bias = params
    normed_one = low(layer_norm(seq_in, attn_gain, attn_shift))
    full_bias = jnp.concatenate([qv_bias[:D], jnp.zeros((D,), jnp.float32), qv_bias[D:]])
    qkv = low(low_back(matmul(normed_one, qkv_weight) + full_bias))
    mixed = low(low_back(attend(qkv[:, :D], qkv[:, D:2 * D], qkv[:, 2 * D:], starts)))
    after_attn = seq_in + low_back(matmul(mixed, out_weight) + out_bias)
    normed_two = low(layer_norm(after_attn, mlp_gain, mlp_shift))
    hidden_pre = low_back(matmul(normed_two, fc_weight) + fc_bias)
    hidden_act = low(gelu_tanh(hidden_pre))
    return after_attn + matmul(hidden_act, proj_weight) + proj_bias

def reference(hidden_in, piece_starts, grad_out, attn_gain, attn_shift, qkv_weight, qv_bias, out_weight, out_bias, mlp_gain, mlp_shift, fc_weight, fc_bias, proj_weight, proj_bias):
    params = tuple((item.astype(jnp.float32) for item in (attn_gain, attn_shift, qkv_weight, qv_bias, out_weight, out_bias, mlp_gain, mlp_shift, fc_weight, fc_bias, proj_weight, proj_bias)))
    group_inputs = hidden_in.astype(jnp.float32).reshape(SEQS // 2, 2, SEQ, D)
    group_starts = piece_starts.reshape(SEQS // 2, 2, PIECES)
    group_cots = grad_out.astype(jnp.float32).reshape(SEQS // 2, 2, SEQ, D)

    def group_step(totals, items):
        inputs_now, starts_now, cots_now = items

        def group_forward(param_set, seq_inputs):
            return jax.vmap(block_forward, in_axes=(None, 0, 0))(param_set, seq_inputs, starts_now)
        outputs_now, pullback = jax.vjp(group_forward, params, inputs_now)
        param_grads, input_grads = pullback(cots_now)
        totals = jax.tree.map(lambda left, right: left + right, totals, param_grads)
        return (totals, (outputs_now.astype(jnp.bfloat16), input_grads))
    zero_grads = tuple((jnp.zeros(item.shape, jnp.float32) for item in params))
    totals, (outputs_all, input_grads_all) = lax.scan(group_step, zero_grads, (group_inputs, group_starts, group_cots))
    return (outputs_all.reshape(SEQS, SEQ, D), input_grads_all.reshape(SEQS, SEQ, D), totals[0], totals[1], totals[2], totals[3], totals[4], totals[5], totals[6], totals[7], totals[8], totals[9], totals[10], totals[11])
```

```python
import jax
import jax.numpy as jnp
from jax import lax
from jax.experimental import pallas as pl
from jax.experimental.pallas import tpu as pltpu
from jax.sharding import PartitionSpec as P

D = 1600
HEADS = 25
HD = 64
FF = 6400
SEQ = 1024
PIECE = 256


EPSILON = 1e-05
MASKED = -1000000000.0
gelu_coeff = 0.7978845608028654
gelu_cubic = 0.044715


def layer_norm(values, gain, shift):
    center = values - jnp.mean(values, axis=-1, keepdims=True)
    inv_std = lax.rsqrt(jnp.mean(center * center, axis=-1, keepdims=True) + EPSILON)
    normed = center * inv_std
    return (normed * gain + shift, normed, inv_std)


def norm_back(upstream, normed, inv_std, gain):
    scaled = upstream * gain
    inner = (
        scaled
        - jnp.mean(scaled, axis=-1, keepdims=True)
        - normed * jnp.mean(scaled * normed, axis=-1, keepdims=True)
    )
    return (inner * inv_std, jnp.sum(upstream * normed, axis=0), jnp.sum(upstream, axis=0))


def gelu_both(values):
    tanh_value = jnp.tanh(gelu_coeff * (values + gelu_cubic * values * values * values))
    result = 0.5 * values * (1.0 + tanh_value)
    slope = 0.5 * (1.0 + tanh_value) + 0.5 * values * (
        1.0 - tanh_value * tanh_value
    ) * gelu_coeff * (1.0 + 3.0 * gelu_cubic * values * values)
    return (result, slope)


def visible(starts, row_pos, key_pos):
    row_in = (
        (row_pos[:, None] >= starts[None, :]) & (row_pos[:, None] < starts[None, :] + PIECE)
    ).astype(jnp.float32)
    key_in = (
        (key_pos[:, None] >= starts[None, :]) & (key_pos[:, None] < starts[None, :] + PIECE)
    ).astype(jnp.float32)
    shared = jnp.dot(row_in, key_in.T, preferred_element_type=jnp.float32) > 0.5
    return (key_pos[None, :] <= row_pos[:, None]) | shared


def head_scores(query_heads, keys_heads, allowed):
    scores = jnp.einsum(
        "thd,shd->hts", query_heads, keys_heads, preferred_element_type=jnp.float32
    ) * HD ** (-0.5)
    return jnp.where(allowed[None], scores, MASKED)


def general_local(
    hidden_in,
    piece_starts,
    grad_out,
    attn_gain,
    attn_shift,
    qkv_weight,
    qv_bias,
    out_weight,
    out_bias,
    mlp_gain,
    mlp_shift,
    fc_weight,
    fc_bias,
    proj_weight,
    proj_bias,
):
    row_count = hidden_in.shape[1]
    shard_rows = attn_gain.shape[0]
    row_pos = lax.axis_index("ctx") * row_count + jnp.arange(row_count, dtype=jnp.int32)
    key_pos = jnp.arange(SEQ, dtype=jnp.int32)
    scale = HD ** (-0.5)
    attn_shards = (attn_gain, attn_shift, qkv_weight, qv_bias, out_weight, out_bias)
    mlp_shards = (mlp_gain, mlp_shift, fc_weight, fc_bias, proj_weight, proj_bias)
    outputs = []
    input_grads = []
    kept_rows = []
    norm_totals = [jnp.zeros((D,), jnp.float32) for index in range(4)]
    for micro_index in range(hidden_in.shape[0]):
        attn_full = (
            lax.all_gather(attn_shards[0], ("dp", "ctx"), axis=0, tiled=True),
            lax.all_gather(attn_shards[1], ("dp", "ctx"), axis=0, tiled=True),
            lax.all_gather(attn_shards[2], ("dp", "ctx"), axis=0, tiled=True),
            lax.all_gather(attn_shards[3], ("dp", "ctx"), axis=0, tiled=True),
            lax.all_gather(attn_shards[4], ("dp", "ctx"), axis=0, tiled=True),
            lax.all_gather(attn_shards[5], ("dp", "ctx"), axis=0, tiled=True),
        )
        mlp_full = (
            lax.all_gather(mlp_shards[0], ("dp", "ctx"), axis=0, tiled=True),
            lax.all_gather(mlp_shards[1], ("dp", "ctx"), axis=0, tiled=True),
            lax.all_gather(mlp_shards[2], ("dp", "ctx"), axis=0, tiled=True),
            lax.all_gather(mlp_shards[3], ("dp", "ctx"), axis=0, tiled=True),
            lax.all_gather(mlp_shards[4], ("dp", "ctx"), axis=0, tiled=True),
            lax.all_gather(mlp_shards[5], ("dp", "ctx"), axis=0, tiled=True),
        )
        gain_one, shift_one, qkv_full, qv_full, out_full, out_bias_full = attn_full
        gain_two, shift_two, fc_full, fc_bias_full, proj_full, proj_bias_full = mlp_full
        tokens = hidden_in[micro_index].astype(jnp.float32)
        starts = piece_starts[micro_index]
        allowed = visible(starts, row_pos, key_pos)
        normed_out, normed_one, inv_one = layer_norm(
            tokens, gain_one.astype(jnp.float32), shift_one.astype(jnp.float32)
        )
        h1_low = normed_out.astype(jnp.bfloat16)
        qv_float = qv_full.astype(jnp.float32)
        full_bias = jnp.concatenate([qv_float[:D], jnp.zeros((D,), jnp.float32), qv_float[D:]])
        qkv_low = (
            jnp.dot(h1_low, qkv_full, preferred_element_type=jnp.float32) + full_bias
        ).astype(jnp.bfloat16)
        query_low = qkv_low[:, :D]
        keys_all, values_all = (
            lax.all_gather(qkv_low[:, D : 2 * D], "ctx", axis=0, tiled=True),
            lax.all_gather(qkv_low[:, 2 * D :], "ctx", axis=0, tiled=True),
        )
        query_heads = query_low.reshape(row_count, HEADS, HD)
        keys_heads = keys_all.reshape(SEQ, HEADS, HD)
        values_heads = values_all.reshape(SEQ, HEADS, HD)
        scores = head_scores(query_heads, keys_heads, allowed)
        top_score = jnp.max(scores, axis=-1, keepdims=True)
        expo = jnp.exp(scores - top_score)
        expo_sum = jnp.sum(expo, axis=-1, keepdims=True)
        probs_low = (expo / expo_sum).astype(jnp.bfloat16)
        log_total = top_score + jnp.log(expo_sum)
        mixed = jnp.einsum(
            "hts,shd->thd", probs_low, values_heads, preferred_element_type=jnp.float32
        )
        attn_low = mixed.reshape(row_count, D).astype(jnp.bfloat16)
        after_attn = (
            tokens
            + jnp.dot(attn_low, out_full, preferred_element_type=jnp.float32)
            + out_bias_full.astype(jnp.float32)
        )
        normed_out_two, normed_two, inv_two = layer_norm(
            after_attn, gain_two.astype(jnp.float32), shift_two.astype(jnp.float32)
        )
        h2_low = normed_out_two.astype(jnp.bfloat16)
        hidden_pre = jnp.dot(
            h2_low, fc_full, preferred_element_type=jnp.float32
        ) + fc_bias_full.astype(jnp.float32)
        hidden_act, hidden_slope = gelu_both(hidden_pre)
        act_low = hidden_act.astype(jnp.bfloat16)
        block_value = (
            after_attn
            + jnp.dot(act_low, proj_full, preferred_element_type=jnp.float32)
            + proj_bias_full.astype(jnp.float32)
        )
        outputs.append(block_value.astype(jnp.bfloat16))
        gain_two_back, fc_back, proj_back = (
            lax.all_gather(mlp_gain, ("dp", "ctx"), axis=0, tiled=True),
            lax.all_gather(fc_weight, ("dp", "ctx"), axis=0, tiled=True),
            lax.all_gather(proj_weight, ("dp", "ctx"), axis=0, tiled=True),
        )
        gain_one_back, qkv_back, out_back = (
            lax.all_gather(attn_gain, ("dp", "ctx"), axis=0, tiled=True),
            lax.all_gather(qkv_weight, ("dp", "ctx"), axis=0, tiled=True),
            lax.all_gather(out_weight, ("dp", "ctx"), axis=0, tiled=True),
        )
        cot_low = grad_out[micro_index]
        grad_act = jnp.einsum("td,fd->tf", cot_low, proj_back, preferred_element_type=jnp.float32)
        grad_pre_low = (grad_act * hidden_slope).astype(jnp.bfloat16)
        grad_h2 = jnp.einsum("tf,df->td", grad_pre_low, fc_back, preferred_element_type=jnp.float32)
        grad_through, grad_gain_two, grad_shift_two = norm_back(
            grad_h2, normed_two, inv_two, gain_two_back.astype(jnp.float32)
        )
        grad_after = grad_through + cot_low.astype(jnp.float32)
        grad_after_low = grad_after.astype(jnp.bfloat16)
        grad_attn_low = jnp.einsum(
            "te,de->td", grad_after_low, out_back, preferred_element_type=jnp.float32
        ).astype(jnp.bfloat16)
        grad_attn_heads = grad_attn_low.reshape(row_count, HEADS, HD)
        again_scores = head_scores(query_heads, keys_heads, allowed)
        probs = jnp.exp(again_scores - log_total)
        probs_again = probs.astype(jnp.bfloat16)
        grad_probs = jnp.einsum(
            "thd,shd->hts", grad_attn_heads, values_heads, preferred_element_type=jnp.float32
        )
        grad_scores_low = (
            probs * (grad_probs - jnp.sum(probs * grad_probs, axis=-1, keepdims=True))
        ).astype(jnp.bfloat16)
        grad_query = (
            jnp.einsum(
                "hts,shd->thd", grad_scores_low, keys_heads, preferred_element_type=jnp.float32
            )
            * scale
        )

        def key_value_term(
            start,
            count,
            grad_scores_low=grad_scores_low,
            probs_again=probs_again,
            query_heads=query_heads,
            grad_attn_heads=grad_attn_heads,
        ):
            grad_k = (
                jnp.einsum(
                    "hts,thd->shd", grad_scores_low, query_heads, preferred_element_type=jnp.float32
                )
                * scale
            )
            grad_v = jnp.einsum(
                "hts,thd->shd", probs_again, grad_attn_heads, preferred_element_type=jnp.float32
            )
            return jnp.concatenate([grad_k.reshape(count, D), grad_v.reshape(count, D)], axis=1)

        kv_summed = lax.psum_scatter(
            key_value_term(jnp.int32(0), lax.axis_size("ctx") * row_count).astype(jnp.bfloat16),
            "ctx",
            scatter_dimension=0,
            tiled=True,
        ).astype(jnp.float32)
        grad_qkv_low = jnp.concatenate(
            [grad_query.reshape(row_count, D), kv_summed], axis=1
        ).astype(jnp.bfloat16)
        grad_h1 = jnp.einsum(
            "te,de->td", grad_qkv_low, qkv_back, preferred_element_type=jnp.float32
        )
        grad_into, grad_gain_one, grad_shift_one = norm_back(
            grad_h1, normed_one, inv_one, gain_one_back.astype(jnp.float32)
        )
        input_grads.append(grad_after + grad_into)
        kept_rows.append(
            (h1_low, grad_qkv_low, attn_low, grad_after_low, h2_low, grad_pre_low, act_low, cot_low)
        )
        norm_totals = [
            norm_totals[0] + grad_gain_one,
            norm_totals[1] + grad_shift_one,
            norm_totals[2] + grad_gain_two,
            norm_totals[3] + grad_shift_two,
        ]
    (
        h1_rows,
        grad_qkv_rows,
        attn_rows,
        grad_after_rows,
        h2_rows,
        grad_pre_rows,
        act_rows,
        cot_rows,
    ) = [jnp.concatenate([item[index] for item in kept_rows], axis=0) for index in range(8)]
    grad_qkv_w = jnp.einsum("td,te->de", h1_rows, grad_qkv_rows, preferred_element_type=jnp.float32)
    grad_out_w = jnp.einsum(
        "td,te->de", attn_rows, grad_after_rows, preferred_element_type=jnp.float32
    )
    attn_matrices = lax.psum_scatter(
        jnp.concatenate([grad_qkv_w, grad_out_w], axis=1),
        ("dp", "ctx"),
        scatter_dimension=0,
        tiled=True,
    )
    grad_fc_w = jnp.einsum("td,tf->df", h2_rows, grad_pre_rows, preferred_element_type=jnp.float32)
    grad_proj_w = jnp.einsum("tf,td->fd", act_rows, cot_rows, preferred_element_type=jnp.float32)
    mlp_matrices = lax.psum_scatter(
        jnp.concatenate(
            [grad_fc_w, grad_proj_w.reshape(lax.axis_size(("dp", "ctx")) * shard_rows, 4 * D)],
            axis=1,
        ),
        ("dp", "ctx"),
        scatter_dimension=0,
        tiled=True,
    )
    column_sums = jnp.sum(grad_qkv_rows, axis=0, dtype=jnp.float32)
    grad_qv_b = jnp.concatenate([column_sums[:D], column_sums[2 * D :]])
    grad_out_b = jnp.sum(grad_after_rows, axis=0, dtype=jnp.float32)
    grad_fc_b = jnp.sum(grad_pre_rows, axis=0, dtype=jnp.float32)
    grad_proj_b = jnp.sum(cot_rows, axis=0, dtype=jnp.float32)
    small_sums = (
        lax.psum_scatter(norm_totals[0], ("dp", "ctx"), scatter_dimension=0, tiled=True),
        lax.psum_scatter(norm_totals[1], ("dp", "ctx"), scatter_dimension=0, tiled=True),
        lax.psum_scatter(grad_qv_b, ("dp", "ctx"), scatter_dimension=0, tiled=True),
        lax.psum_scatter(grad_out_b, ("dp", "ctx"), scatter_dimension=0, tiled=True),
        lax.psum_scatter(norm_totals[2], ("dp", "ctx"), scatter_dimension=0, tiled=True),
        lax.psum_scatter(norm_totals[3], ("dp", "ctx"), scatter_dimension=0, tiled=True),
        lax.psum_scatter(grad_fc_b, ("dp", "ctx"), scatter_dimension=0, tiled=True),
        lax.psum_scatter(grad_proj_b, ("dp", "ctx"), scatter_dimension=0, tiled=True),
    )
    grad_qkv_shard = attn_matrices[:, : 3 * D]
    grad_out_shard = attn_matrices[:, 3 * D :]
    grad_fc_shard = mlp_matrices[:, :FF]
    grad_proj_shard = mlp_matrices[:, FF:].reshape(4 * shard_rows, D)
    summed = (
        lax.psum(small_sums[0].astype(jnp.bfloat16), "rep").astype(jnp.float32),
        lax.psum(small_sums[1].astype(jnp.bfloat16), "rep").astype(jnp.float32),
        lax.psum(grad_qkv_shard.astype(jnp.bfloat16), "rep").astype(jnp.float32),
        lax.psum(small_sums[2].astype(jnp.bfloat16), "rep").astype(jnp.float32),
        lax.psum(grad_out_shard.astype(jnp.bfloat16), "rep").astype(jnp.float32),
        lax.psum(small_sums[3].astype(jnp.bfloat16), "rep").astype(jnp.float32),
        lax.psum(small_sums[4].astype(jnp.bfloat16), "rep").astype(jnp.float32),
        lax.psum(small_sums[5].astype(jnp.bfloat16), "rep").astype(jnp.float32),
        lax.psum(grad_fc_shard.astype(jnp.bfloat16), "rep").astype(jnp.float32),
        lax.psum(small_sums[6].astype(jnp.bfloat16), "rep").astype(jnp.float32),
        lax.psum(grad_proj_shard.astype(jnp.bfloat16), "rep").astype(jnp.float32),
        lax.psum(small_sums[7].astype(jnp.bfloat16), "rep").astype(jnp.float32),
    )
    return (
        jnp.stack(outputs),
        jnp.stack(input_grads),
        summed[0],
        summed[1],
        summed[2],
        summed[3],
        summed[4],
        summed[5],
        summed[6],
        summed[7],
        summed[8],
        summed[9],
        summed[10],
        summed[11],
    )


LANES = 128


def over_core(value):
    return lax.ppermute(value, "rep", [(0, 1), (1, 0), (2, 3), (3, 2)])


def over_x(value):
    return lax.ppermute(value, "rep", [(0, 2), (2, 0), (1, 3), (3, 1)])


def over_y(value):
    return lax.ppermute(value, "dp", [(0, 1), (1, 0)])


def ordered(first_is_mine, mine, other):
    return jnp.stack(
        [jnp.where(first_is_mine, mine, other), jnp.where(first_is_mine, other, mine)]
    )


def mxu(left, right, dims=((1,), (0,))):
    return lax.dot_general(left, right, (dims, ((), ())), preferred_element_type=jnp.float32)


def attend_forward_kernel(limit_ref, q_ref, k_ref, v_t_ref, o_ref, lse_ref):
    pair = pl.program_id(0)
    width = q_ref.shape[0] // 2
    lane = lax.broadcasted_iota(jnp.int32, (1, LANES), 1)
    valid = lane < D - pair * LANES
    queries = jnp.where(valid, q_ref[...], 0) * jnp.asarray(HD ** (-0.5), q_ref.dtype)
    keys = jnp.where(valid, k_ref[...], 0)
    for part in range(2):
        rows = slice(part * width, (part + 1) * width)
        first, count = KEY_SPANS[part]
        limit = limit_ref[:, rows]
        mixed = []
        for head in range(2):
            own = (lane >= head * HD) & (lane < (head + 1) * HD)
            scores = mxu(keys[:count], jnp.where(own, queries[rows], 0), ((1,), (1,)))
            position = first + lax.broadcasted_iota(jnp.int32, (count - first, width), 0)
            tail = jnp.where(position < limit, scores[first:], MASKED)
            scores = tail if first == 0 else jnp.concatenate([scores[:first], tail], axis=0)
            top = jnp.max(scores, axis=0, keepdims=True)
            expo = jnp.exp(scores - top)
            total = jnp.sum(expo, axis=0, keepdims=True)
            values = v_t_ref[head * HD : (head + 1) * HD, :count]
            mixed.append(mxu(values, expo.astype(jnp.bfloat16)) / total)
            lse_ref[0, head : head + 1, rows] = top + jnp.log(total)
        o_ref[rows, :] = jnp.concatenate(mixed, axis=0).T.astype(o_ref.dtype)


def attend_backward_kernel(
    limit_ref,
    q_ref,
    k_ref,
    k_t_ref,
    v_ref,
    grad_ref,
    lse_ref,
    dq_ref,
    dk_ref,
    dv_ref,
    dk_sum,
    dv_sum,
):
    pair = pl.program_id(0)
    width = q_ref.shape[0] // 2
    lane = lax.broadcasted_iota(jnp.int32, (1, LANES), 1)
    valid = lane < D - pair * LANES
    queries = jnp.where(valid, q_ref[...], 0) * jnp.asarray(HD ** (-0.5), q_ref.dtype)
    grads = jnp.where(valid, grad_ref[...], 0)
    keys = jnp.where(valid, k_ref[...], 0)
    values = jnp.where(valid, v_ref[...], 0)
    dk_sum[...] = jnp.zeros_like(dk_sum)
    dv_sum[...] = jnp.zeros_like(dv_sum)
    for part in range(2):
        rows = slice(part * width, (part + 1) * width)
        first, count = KEY_SPANS[part]
        limit = limit_ref[:, rows]
        grad_q = []
        for head in range(2):
            own = (lane >= head * HD) & (lane < (head + 1) * HD)
            queries_own = jnp.where(own, queries[rows], 0)
            grads_own = jnp.where(own, grads[rows], 0)
            scores = mxu(keys[:count], queries_own, ((1,), (1,)))
            position = first + lax.broadcasted_iota(jnp.int32, (count - first, width), 0)
            tail = jnp.where(position < limit, scores[first:], MASKED)
            scores = tail if first == 0 else jnp.concatenate([scores[:first], tail], axis=0)
            probs = jnp.exp(scores - lse_ref[0, head : head + 1, rows])
            grad_probs = mxu(values[:count], grads_own, ((1,), (1,)))
            inner = jnp.sum(probs * grad_probs, axis=0, keepdims=True)
            grad_scores = (probs * (grad_probs - inner)).astype(jnp.bfloat16)
            grad_q.append(mxu(k_t_ref[head * HD : (head + 1) * HD, :count], grad_scores))
            dk_sum[:count, :] += mxu(grad_scores, queries_own)
            dv_sum[:count, :] += mxu(probs.astype(jnp.bfloat16), grads_own)
        grad_q = jnp.concatenate(grad_q, axis=0) * HD ** (-0.5)
        dq_ref[rows, :] = grad_q.T.astype(dq_ref.dtype)
    dk_ref[...] = dk_sum[...].astype(dk_ref.dtype)
    dv_ref[...] = dv_sum[...].astype(dv_ref.dtype)


PAIRS = -(-D // LANES)
KEY_SPANS = ((0, 640), (512, 1024))


def by_columns(rows):
    return pl.BlockSpec((rows, LANES), lambda pair: (0, pair))


def by_rows(columns):
    return pl.BlockSpec((LANES, columns), lambda pair: (pair, 0))


def attend_forward(limit, q, k, v_t):
    rows, keys = q.shape[0], k.shape[0]
    return pl.pallas_call(
        attend_forward_kernel,
        grid=(PAIRS,),
        in_specs=[
            pl.BlockSpec((1, rows), lambda pair: (0, 0)),
            by_columns(rows),
            by_columns(keys),
            by_rows(keys),
        ],
        out_specs=[by_columns(rows), pl.BlockSpec((1, 2, rows), lambda pair: (pair, 0, 0))],
        out_shape=[
            jax.ShapeDtypeStruct((rows, D), jnp.bfloat16),
            jax.ShapeDtypeStruct((PAIRS, 2, rows), jnp.float32),
        ],
        cost_estimate=pl.CostEstimate(
            flops=4 * rows * keys * D, transcendentals=rows * keys * HEADS, bytes_accessed=8 * keys * D
        ),
        compiler_params=pltpu.CompilerParams(vmem_limit_bytes=48 << 20),
        name="attend_forward",
    )(limit, q, k, v_t)


def attend_backward(limit, q, k, k_t, v, grad, lse):
    rows, keys = q.shape[0], k.shape[0]
    return pl.pallas_call(
        attend_backward_kernel,
        grid=(PAIRS,),
        in_specs=[
            pl.BlockSpec((1, rows), lambda pair: (0, 0)),
            by_columns(rows),
            by_columns(keys),
            by_rows(keys),
            by_columns(keys),
            by_columns(rows),
            pl.BlockSpec((1, 2, rows), lambda pair: (pair, 0, 0)),
        ],
        out_specs=[by_columns(rows), by_columns(keys), by_columns(keys)],
        out_shape=[
            jax.ShapeDtypeStruct((rows, D), jnp.bfloat16),
            jax.ShapeDtypeStruct((keys, D), jnp.bfloat16),
            jax.ShapeDtypeStruct((keys, D), jnp.bfloat16),
        ],
        scratch_shapes=[pltpu.VMEM((keys, LANES), jnp.float32), pltpu.VMEM((keys, LANES), jnp.float32)],
        cost_estimate=pl.CostEstimate(
            flops=10 * rows * keys * D, transcendentals=rows * keys * HEADS, bytes_accessed=16 * keys * D
        ),
        compiler_params=pltpu.CompilerParams(vmem_limit_bytes=48 << 20),
        name="attend_backward",
    )(limit, q, k, k_t, v, grad, lse)


def sequence_local(
    hidden_in,
    piece_starts,
    grad_out,
    attn_gain,
    attn_shift,
    qkv_weight,
    qv_bias,
    out_weight,
    out_bias,
    mlp_gain,
    mlp_shift,
    fc_weight,
    fc_bias,
    proj_weight,
    proj_bias,
):
    rep, dp, ctx = (lax.axis_index(name) for name in ("rep", "dp", "ctx"))
    chip_x, core = rep // 2, rep % 2
    chips, shards = lax.axis_size("ctx"), lax.axis_size(("dp", "ctx"))
    seqs, block, _ = hidden_in.shape
    half = block // 2
    rows = chips * half
    shard_rows = D // shards
    f32, low = jnp.float32, jnp.bfloat16
    core_low, x_low, y_low = core == 0, chip_x == 0, dp == 0
    half_of = lambda index: (core + index) % 2

    def to_sequence(value):
        halves = value.reshape(seqs, 2, half, D)
        mine = half_of(ctx)
        kept = lax.dynamic_index_in_dim(halves, mine, 1, keepdims=False)
        came = over_core(lax.dynamic_index_in_dim(halves, 1 - mine, 1, keepdims=False))
        every = ordered(core_low, kept, came).reshape(chips, half, D)
        return lax.all_to_all(every, "ctx", 0, 0, tiled=True).reshape(rows, D)

    def from_sequence(value):
        every = lax.all_to_all(value.reshape(chips, half, D), "ctx", 0, 0, tiled=True)
        every = every.reshape(2, seqs, half, D)
        kept = lax.dynamic_index_in_dim(every, core, 0, keepdims=False)
        came = over_core(lax.dynamic_index_in_dim(every, 1 - core, 0, keepdims=False))
        both = ordered(half_of(ctx) == 0, kept, came)
        return both.transpose(1, 0, 2, 3).reshape(seqs, block, D)

    def interleave(mine, other):
        mine, other = mine.reshape(chips, half, D), other.reshape(chips, half, D)
        first = (half_of(jnp.arange(chips)) == 0)[:, None, None]
        return jnp.stack(
            [jnp.where(first, mine, other), jnp.where(first, other, mine)], axis=1
        ).reshape(2 * rows, D)

    def split_rows(value):
        value = value.reshape(chips, 2, half, D)
        first = (half_of(jnp.arange(chips)) == 0)[:, None, None]
        return (
            jnp.where(first, value[:, 0], value[:, 1]).reshape(rows, D),
            jnp.where(first, value[:, 1], value[:, 0]).reshape(rows, D),
        )

    def gather_shared(shard):
        mine = lax.all_gather(shard, "ctx", axis=0, tiled=True)
        count = mine.shape[0] // 2
        near = over_y(lax.dynamic_slice_in_dim(mine, chip_x * count, count, 0))
        far = over_x(near)
        other = ordered(x_low, near, far).reshape(mine.shape)
        return ordered(y_low, mine, other).reshape(2 * mine.shape[0], D)

    def gather_own(shard):
        mine = lax.all_gather(shard, "ctx", axis=0, tiled=True)
        other = over_y(mine)
        return ordered(y_low, mine, other).reshape(2 * mine.shape[0], D)

    small = jnp.concatenate(
        [attn_gain, attn_shift, qv_bias, out_bias, mlp_gain, mlp_shift, fc_bias, proj_bias]
    )
    small = lax.all_gather(small[None], ("dp", "ctx"), axis=0, tiled=True).astype(f32)
    parts, at = [], 0
    for item in (attn_gain, attn_shift, qv_bias, out_bias, mlp_gain, mlp_shift, fc_bias, proj_bias):
        parts.append(small[:, at : at + item.shape[0]].reshape(-1))
        at += item.shape[0]
    gain_one, shift_one, qv_full, out_bias_full, gain_two, shift_two, fc_bias_full, proj_bias_full = parts
    query_bias, value_bias = qv_full[:D], qv_full[D:]
    fc_bias_mine = lax.dynamic_index_in_dim(
        fc_bias_full.reshape(shards, 4, shard_rows), rep, 1, keepdims=False
    ).reshape(D)

    q_or_v = gather_shared(jnp.where(core_low, qkv_weight[:, :D], qkv_weight[:, 2 * D :]))
    k_or_out = gather_shared(jnp.where(core_low, qkv_weight[:, D : 2 * D], out_weight))
    v_or_q, out_or_k = over_core(q_or_v), over_core(k_or_out)
    fc_mine = gather_own(
        lax.dynamic_index_in_dim(
            fc_weight.reshape(shard_rows, shards, 4, shard_rows), rep, 2, keepdims=False
        ).reshape(shard_rows, D)
    )
    proj_mine = gather_own(
        lax.dynamic_index_in_dim(proj_weight.reshape(4, shard_rows, D), rep, 0, keepdims=False)
    )
    key_weight = jnp.where(core_low, k_or_out, out_or_k)
    out_full = jnp.where(core_low, out_or_k, k_or_out)

    tokens_low = to_sequence(hidden_in)
    cot_low = to_sequence(grad_out)
    every_starts = ordered(core_low, piece_starts, over_core(piece_starts)).reshape(chips, -1)
    starts = lax.dynamic_index_in_dim(every_starts, ctx, 0, keepdims=False)
    block_index = jnp.arange(chips)
    row_pos = (
        (block_index * block + half_of(block_index) * half)[:, None] + jnp.arange(half)[None, :]
    ).reshape(rows)
    inside = (row_pos[:, None] >= starts[None, :]) & (row_pos[:, None] < starts[None, :] + PIECE)
    limit = jnp.maximum(row_pos + 1, jnp.max(jnp.where(inside, starts[None, :] + PIECE, 0), axis=1))
    limit = limit.astype(jnp.int32)[None, :]

    tokens = tokens_low.astype(f32)
    normed_out, normed_one, inv_one = layer_norm(tokens, gain_one, shift_one)
    h1_low = normed_out.astype(low)
    bias_a = jnp.where(core_low, query_bias, value_bias)
    bias_b = jnp.where(core_low, value_bias, query_bias)
    result_a = (mxu(h1_low, q_or_v) + bias_a).astype(low)
    result_b = (mxu(h1_low, v_or_q) + bias_b).astype(low)
    query_low = jnp.where(core_low, result_a, result_b)
    value_low = jnp.where(core_low, result_b, result_a)
    key_low = mxu(h1_low, key_weight).astype(low)
    keys = interleave(key_low, over_core(key_low))
    values = interleave(value_low, over_core(value_low))
    attn_low, lse = attend_forward(limit, query_low, keys, values.T)
    after_attn = tokens + mxu(attn_low, out_full) + out_bias_full
    normed_out_two, normed_two, inv_two = layer_norm(after_attn, gain_two, shift_two)
    h2_low = normed_out_two.astype(low)

    def spread(value):
        chip = jnp.concatenate([value, over_x(value)], axis=0)
        return jnp.concatenate([chip, over_core(chip)], axis=0)

    def collect(value):
        terms = value.astype(low)
        pair = terms[: 2 * rows].astype(f32) + over_core(terms[2 * rows :]).astype(f32)
        return pair[:rows] + over_x(pair[rows:].astype(low)).astype(f32)

    h2_all = spread(h2_low)
    cot_all = spread(cot_low)
    hidden_pre = mxu(h2_all, fc_mine) + fc_bias_mine
    hidden_act, hidden_slope = gelu_both(hidden_pre)
    act_low = hidden_act.astype(low)
    block_value = (after_attn + collect(mxu(act_low, proj_mine)) + proj_bias_full).astype(low)

    grad_act = mxu(cot_all, proj_mine, ((1,), (1,)))
    grad_pre_low = (grad_act * hidden_slope).astype(low)
    grad_proj_mine = mxu(act_low, cot_all, ((0,), (0,)))
    grad_fc_mine = mxu(h2_all, grad_pre_low, ((0,), (0,)))
    grad_h2 = collect(mxu(grad_pre_low, fc_mine, ((1,), (1,))))
    grad_through, grad_gain_two, grad_shift_two = norm_back(grad_h2, normed_two, inv_two, gain_two)
    grad_after = grad_through + cot_low.astype(f32)
    grad_after_low = grad_after.astype(low)

    grad_attn_low = mxu(grad_after_low, out_full, ((1,), (1,))).astype(low)
    grad_query, grad_keys, grad_values = attend_backward(
        limit, query_low, keys, keys.T, values, grad_attn_low, lse
    )

    def own_rows(value):
        mine, other = split_rows(value)
        return (mine.astype(f32) + over_core(other).astype(f32)).astype(low)

    grad_key, grad_value = own_rows(grad_keys), own_rows(grad_values)
    grad_a = jnp.where(core_low, grad_query, grad_value)
    grad_b = jnp.where(core_low, grad_value, grad_query)
    grad_h1 = (
        mxu(grad_a, q_or_v, ((1,), (1,)))
        + mxu(grad_b, v_or_q, ((1,), (1,)))
        + mxu(grad_key, key_weight, ((1,), (1,)))
    )
    grad_into, grad_gain_one, grad_shift_one = norm_back(grad_h1, normed_one, inv_one, gain_one)
    input_grad = from_sequence((grad_after + grad_into).astype(low)).astype(f32)
    block_out = from_sequence(block_value)

    h1_chip = jnp.concatenate([h1_low, over_core(h1_low)], axis=0)
    attn_chip = jnp.concatenate([attn_low, over_core(attn_low)], axis=0)
    right_a = jnp.concatenate([grad_a, over_core(grad_b)], axis=0)
    right_b = jnp.concatenate(
        [
            jnp.where(core_low, grad_key, grad_after_low),
            over_core(jnp.where(core_low, grad_after_low, grad_key)),
        ],
        axis=0,
    )
    left_b = jnp.where(core_low, h1_chip, attn_chip)
    term_a = mxu(h1_chip, right_a, ((0,), (0,))).astype(low)
    term_b = mxu(left_b, right_b, ((0,), (0,))).astype(low)

    def finish(value):
        return lax.psum_scatter(value, "ctx", scatter_dimension=0, tiled=True)

    def sum_own(value):
        both = value.astype(low).reshape(2, -1, D)
        kept = lax.dynamic_index_in_dim(both, dp, 0, keepdims=False)
        came = over_y(lax.dynamic_index_in_dim(both, 1 - dp, 0, keepdims=False))
        return finish((kept.astype(f32) + came.astype(f32)).astype(low))

    def sum_shared(first, second):
        quarter = D // 4
        both = jnp.stack([first, second]).reshape(2, 2, 2, quarter, D)
        kept_x = lax.dynamic_index_in_dim(both[:, :, 0], chip_x, 0, keepdims=False)
        came_x = over_x(lax.dynamic_index_in_dim(both[:, :, 0], 1 - chip_x, 0, keepdims=False))
        kept_y = lax.dynamic_index_in_dim(both[:, :, 1], dp, 1, keepdims=False)
        came_y = over_y(lax.dynamic_index_in_dim(both[:, :, 1], 1 - dp, 1, keepdims=False))
        sum_x = (kept_x.astype(f32) + came_x.astype(f32)).astype(low)
        sum_y = (kept_y.astype(f32) + came_y.astype(f32)).astype(low)
        last_x = lax.dynamic_index_in_dim(sum_x, dp, 0, keepdims=False).astype(f32) + over_y(
            lax.dynamic_index_in_dim(sum_x, 1 - dp, 0, keepdims=False)
        ).astype(f32)
        last_y = lax.dynamic_index_in_dim(sum_y, chip_x, 0, keepdims=False).astype(f32) + over_x(
            lax.dynamic_index_in_dim(sum_y, 1 - chip_x, 0, keepdims=False)
        ).astype(f32)
        return finish(jnp.concatenate([last_x, last_y], axis=0).astype(low))

    def share(value):
        pair = ordered(x_low, value, over_x(value))
        return ordered(core_low, pair, over_core(pair)).reshape((4,) + value.shape)

    attn_quarters = share(sum_shared(term_a, term_b)).astype(f32)
    grad_qkv_shard = jnp.concatenate([attn_quarters[0], attn_quarters[1], attn_quarters[2]], axis=1)
    grad_out_shard = attn_quarters[3]
    fc_quarters = share(sum_own(grad_fc_mine)).astype(f32)
    grad_fc_shard = (
        fc_quarters.reshape(2, 2, shard_rows, shards, shard_rows)
        .transpose(2, 3, 1, 0, 4)
        .reshape(shard_rows, FF)
    )
    proj_quarters = share(sum_own(grad_proj_mine)).astype(f32)
    grad_proj_shard = (
        proj_quarters.reshape(2, 2, shard_rows, D).transpose(1, 0, 2, 3).reshape(4 * shard_rows, D)
    )

    fc_bias_part = jnp.where(
        jnp.arange(4)[None, :, None] == rep,
        jnp.sum(grad_pre_low, axis=0, dtype=f32).reshape(shards, 1, shard_rows),
        0.0,
    )
    sums = [
        grad_gain_one,
        grad_shift_one,
        jnp.concatenate(
            [jnp.sum(grad_query, axis=0, dtype=f32), jnp.sum(grad_value, axis=0, dtype=f32)]
        ),
        jnp.sum(grad_after_low, axis=0, dtype=f32),
        grad_gain_two,
        grad_shift_two,
        fc_bias_part,
        jnp.sum(cot_low, axis=0, dtype=f32),
    ]
    table = jnp.concatenate([item.reshape(shards, -1) for item in sums], axis=1)
    table = lax.psum(table, ("rep", "dp", "ctx"))
    mine = lax.dynamic_index_in_dim(table, dp * chips + ctx, 0, keepdims=False)
    small_out, at = [], 0
    for item in sums:
        count = item.size // shards
        small_out.append(mine[at : at + count])
        at += count
    return (
        block_out,
        input_grad,
        small_out[0],
        small_out[1],
        grad_qkv_shard,
        small_out[2],
        grad_out_shard,
        small_out[3],
        small_out[4],
        small_out[5],
        grad_fc_shard,
        small_out[6],
        grad_proj_shard,
        small_out[7],
    )


def local(hidden_in, *rest):
    seqs, block, _ = hidden_in.shape
    sizes = tuple(lax.axis_size(name) for name in ("rep", "dp", "ctx"))
    if sizes[:2] == (4, 2) and 2 * seqs == sizes[2] and sizes[2] * block == SEQ and block == PIECE:
        return sequence_local(hidden_in, *rest)
    return general_local(hidden_in, *rest)


def solution(mesh):
    placed = (
        P(("rep", "dp"), "ctx", None),
        P(("rep", "dp"), None),
        P(("rep", "dp"), "ctx", None),
        P(("dp", "ctx")),
        P(("dp", "ctx")),
        P(("dp", "ctx"), None),
        P(("dp", "ctx")),
        P(("dp", "ctx"), None),
        P(("dp", "ctx")),
        P(("dp", "ctx")),
        P(("dp", "ctx")),
        P(("dp", "ctx"), None),
        P(("dp", "ctx")),
        P(("dp", "ctx"), None),
        P(("dp", "ctx")),
    )
    return jax.shard_map(
        local,
        mesh=mesh,
        in_specs=placed,
        out_specs=(
            P(("rep", "dp"), "ctx", None),
            P(("rep", "dp"), "ctx", None),
            P(("dp", "ctx")),
            P(("dp", "ctx")),
            P(("dp", "ctx"), None),
            P(("dp", "ctx")),
            P(("dp", "ctx"), None),
            P(("dp", "ctx")),
            P(("dp", "ctx")),
            P(("dp", "ctx")),
            P(("dp", "ctx"), None),
            P(("dp", "ctx")),
            P(("dp", "ctx"), None),
            P(("dp", "ctx")),
        ),
        check_vma=False,
    )
```

```python
import jax
import jax.numpy as jnp
from jax import lax
from jax.experimental import pallas as pl
from jax.experimental.pallas import tpu as pltpu
from jax.sharding import PartitionSpec as P

D = 1600
HEADS = 25
HD = 64
FF = 6400
SEQ = 1024
PIECE = 256


EPSILON = 1e-05
MASKED = -1000000000.0
gelu_coeff = 0.7978845608028654
gelu_cubic = 0.044715


def layer_norm(values, gain, shift):
    center = values - jnp.mean(values, axis=-1, keepdims=True)
    inv_std = lax.rsqrt(jnp.mean(center * center, axis=-1, keepdims=True) + EPSILON)
    normed = center * inv_std
    return (normed * gain + shift, normed, inv_std)


def norm_back(upstream, normed, inv_std, gain):
    scaled = upstream * gain
    inner = (
        scaled
        - jnp.mean(scaled, axis=-1, keepdims=True)
        - normed * jnp.mean(scaled * normed, axis=-1, keepdims=True)
    )
    return (inner * inv_std, jnp.sum(upstream * normed, axis=0), jnp.sum(upstream, axis=0))


def gelu_both(values):
    tanh_value = jnp.tanh(gelu_coeff * (values + gelu_cubic * values * values * values))
    result = 0.5 * values * (1.0 + tanh_value)
    slope = 0.5 * (1.0 + tanh_value) + 0.5 * values * (
        1.0 - tanh_value * tanh_value
    ) * gelu_coeff * (1.0 + 3.0 * gelu_cubic * values * values)
    return (result, slope)


def visible(starts, row_pos, key_pos):
    row_in = (
        (row_pos[:, None] >= starts[None, :]) & (row_pos[:, None] < starts[None, :] + PIECE)
    ).astype(jnp.float32)
    key_in = (
        (key_pos[:, None] >= starts[None, :]) & (key_pos[:, None] < starts[None, :] + PIECE)
    ).astype(jnp.float32)
    shared = jnp.dot(row_in, key_in.T, preferred_element_type=jnp.float32) > 0.5
    return (key_pos[None, :] <= row_pos[:, None]) | shared


def head_scores(query_heads, keys_heads, allowed):
    scores = jnp.einsum(
        "thd,shd->hts", query_heads, keys_heads, preferred_element_type=jnp.float32
    ) * HD ** (-0.5)
    return jnp.where(allowed[None], scores, MASKED)


def general_local(
    hidden_in,
    piece_starts,
    grad_out,
    attn_gain,
    attn_shift,
    qkv_weight,
    qv_bias,
    out_weight,
    out_bias,
    mlp_gain,
    mlp_shift,
    fc_weight,
    fc_bias,
    proj_weight,
    proj_bias,
):
    row_count = hidden_in.shape[1]
    shard_rows = attn_gain.shape[0]
    row_pos = lax.axis_index("ctx") * row_count + jnp.arange(row_count, dtype=jnp.int32)
    key_pos = jnp.arange(SEQ, dtype=jnp.int32)
    scale = HD ** (-0.5)
    attn_shards = (attn_gain, attn_shift, qkv_weight, qv_bias, out_weight, out_bias)
    mlp_shards = (mlp_gain, mlp_shift, fc_weight, fc_bias, proj_weight, proj_bias)
    outputs = []
    input_grads = []
    kept_rows = []
    norm_totals = [jnp.zeros((D,), jnp.float32) for index in range(4)]
    for micro_index in range(hidden_in.shape[0]):
        attn_full = (
            lax.all_gather(attn_shards[0], ("dp", "ctx"), axis=0, tiled=True),
            lax.all_gather(attn_shards[1], ("dp", "ctx"), axis=0, tiled=True),
            lax.all_gather(attn_shards[2], ("dp", "ctx"), axis=0, tiled=True),
            lax.all_gather(attn_shards[3], ("dp", "ctx"), axis=0, tiled=True),
            lax.all_gather(attn_shards[4], ("dp", "ctx"), axis=0, tiled=True),
            lax.all_gather(attn_shards[5], ("dp", "ctx"), axis=0, tiled=True),
        )
        mlp_full = (
            lax.all_gather(mlp_shards[0], ("dp", "ctx"), axis=0, tiled=True),
            lax.all_gather(mlp_shards[1], ("dp", "ctx"), axis=0, tiled=True),
            lax.all_gather(mlp_shards[2], ("dp", "ctx"), axis=0, tiled=True),
            lax.all_gather(mlp_shards[3], ("dp", "ctx"), axis=0, tiled=True),
            lax.all_gather(mlp_shards[4], ("dp", "ctx"), axis=0, tiled=True),
            lax.all_gather(mlp_shards[5], ("dp", "ctx"), axis=0, tiled=True),
        )
        gain_one, shift_one, qkv_full, qv_full, out_full, out_bias_full = attn_full
        gain_two, shift_two, fc_full, fc_bias_full, proj_full, proj_bias_full = mlp_full
        tokens = hidden_in[micro_index].astype(jnp.float32)
        starts = piece_starts[micro_index]
        allowed = visible(starts, row_pos, key_pos)
        normed_out, normed_one, inv_one = layer_norm(
            tokens, gain_one.astype(jnp.float32), shift_one.astype(jnp.float32)
        )
        h1_low = normed_out.astype(jnp.bfloat16)
        qv_float = qv_full.astype(jnp.float32)
        full_bias = jnp.concatenate([qv_float[:D], jnp.zeros((D,), jnp.float32), qv_float[D:]])
        qkv_low = (
            jnp.dot(h1_low, qkv_full, preferred_element_type=jnp.float32) + full_bias
        ).astype(jnp.bfloat16)
        query_low = qkv_low[:, :D]
        keys_all, values_all = (
            lax.all_gather(qkv_low[:, D : 2 * D], "ctx", axis=0, tiled=True),
            lax.all_gather(qkv_low[:, 2 * D :], "ctx", axis=0, tiled=True),
        )
        query_heads = query_low.reshape(row_count, HEADS, HD)
        keys_heads = keys_all.reshape(SEQ, HEADS, HD)
        values_heads = values_all.reshape(SEQ, HEADS, HD)
        scores = head_scores(query_heads, keys_heads, allowed)
        top_score = jnp.max(scores, axis=-1, keepdims=True)
        expo = jnp.exp(scores - top_score)
        expo_sum = jnp.sum(expo, axis=-1, keepdims=True)
        probs_low = (expo / expo_sum).astype(jnp.bfloat16)
        log_total = top_score + jnp.log(expo_sum)
        mixed = jnp.einsum(
            "hts,shd->thd", probs_low, values_heads, preferred_element_type=jnp.float32
        )
        attn_low = mixed.reshape(row_count, D).astype(jnp.bfloat16)
        after_attn = (
            tokens
            + jnp.dot(attn_low, out_full, preferred_element_type=jnp.float32)
            + out_bias_full.astype(jnp.float32)
        )
        normed_out_two, normed_two, inv_two = layer_norm(
            after_attn, gain_two.astype(jnp.float32), shift_two.astype(jnp.float32)
        )
        h2_low = normed_out_two.astype(jnp.bfloat16)
        hidden_pre = jnp.dot(
            h2_low, fc_full, preferred_element_type=jnp.float32
        ) + fc_bias_full.astype(jnp.float32)
        hidden_act, hidden_slope = gelu_both(hidden_pre)
        act_low = hidden_act.astype(jnp.bfloat16)
        block_value = (
            after_attn
            + jnp.dot(act_low, proj_full, preferred_element_type=jnp.float32)
            + proj_bias_full.astype(jnp.float32)
        )
        outputs.append(block_value.astype(jnp.bfloat16))
        gain_two_back, fc_back, proj_back = (
            lax.all_gather(mlp_gain, ("dp", "ctx"), axis=0, tiled=True),
            lax.all_gather(fc_weight, ("dp", "ctx"), axis=0, tiled=True),
            lax.all_gather(proj_weight, ("dp", "ctx"), axis=0, tiled=True),
        )
        gain_one_back, qkv_back, out_back = (
            lax.all_gather(attn_gain, ("dp", "ctx"), axis=0, tiled=True),
            lax.all_gather(qkv_weight, ("dp", "ctx"), axis=0, tiled=True),
            lax.all_gather(out_weight, ("dp", "ctx"), axis=0, tiled=True),
        )
        cot_low = grad_out[micro_index]
        grad_act = jnp.einsum("td,fd->tf", cot_low, proj_back, preferred_element_type=jnp.float32)
        grad_pre_low = (grad_act * hidden_slope).astype(jnp.bfloat16)
        grad_h2 = jnp.einsum("tf,df->td", grad_pre_low, fc_back, preferred_element_type=jnp.float32)
        grad_through, grad_gain_two, grad_shift_two = norm_back(
            grad_h2, normed_two, inv_two, gain_two_back.astype(jnp.float32)
        )
        grad_after = grad_through + cot_low.astype(jnp.float32)
        grad_after_low = grad_after.astype(jnp.bfloat16)
        grad_attn_low = jnp.einsum(
            "te,de->td", grad_after_low, out_back, preferred_element_type=jnp.float32
        ).astype(jnp.bfloat16)
        grad_attn_heads = grad_attn_low.reshape(row_count, HEADS, HD)
        again_scores = head_scores(query_heads, keys_heads, allowed)
        probs = jnp.exp(again_scores - log_total)
        probs_again = probs.astype(jnp.bfloat16)
        grad_probs = jnp.einsum(
            "thd,shd->hts", grad_attn_heads, values_heads, preferred_element_type=jnp.float32
        )
        grad_scores_low = (
            probs * (grad_probs - jnp.sum(probs * grad_probs, axis=-1, keepdims=True))
        ).astype(jnp.bfloat16)
        grad_query = (
            jnp.einsum(
                "hts,shd->thd", grad_scores_low, keys_heads, preferred_element_type=jnp.float32
            )
            * scale
        )

        def key_value_term(
            start,
            count,
            grad_scores_low=grad_scores_low,
            probs_again=probs_again,
            query_heads=query_heads,
            grad_attn_heads=grad_attn_heads,
        ):
            grad_k = (
                jnp.einsum(
                    "hts,thd->shd", grad_scores_low, query_heads, preferred_element_type=jnp.float32
                )
                * scale
            )
            grad_v = jnp.einsum(
                "hts,thd->shd", probs_again, grad_attn_heads, preferred_element_type=jnp.float32
            )
            return jnp.concatenate([grad_k.reshape(count, D), grad_v.reshape(count, D)], axis=1)

        kv_summed = lax.psum_scatter(
            key_value_term(jnp.int32(0), lax.axis_size("ctx") * row_count).astype(jnp.bfloat16),
            "ctx",
            scatter_dimension=0,
            tiled=True,
        ).astype(jnp.float32)
        grad_qkv_low = jnp.concatenate(
            [grad_query.reshape(row_count, D), kv_summed], axis=1
        ).astype(jnp.bfloat16)
        grad_h1 = jnp.einsum(
            "te,de->td", grad_qkv_low, qkv_back, preferred_element_type=jnp.float32
        )
        grad_into, grad_gain_one, grad_shift_one = norm_back(
            grad_h1, normed_one, inv_one, gain_one_back.astype(jnp.float32)
        )
        input_grads.append(grad_after + grad_into)
        kept_rows.append(
            (h1_low, grad_qkv_low, attn_low, grad_after_low, h2_low, grad_pre_low, act_low, cot_low)
        )
        norm_totals = [
            norm_totals[0] + grad_gain_one,
            norm_totals[1] + grad_shift_one,
            norm_totals[2] + grad_gain_two,
            norm_totals[3] + grad_shift_two,
        ]
    (
        h1_rows,
        grad_qkv_rows,
        attn_rows,
        grad_after_rows,
        h2_rows,
        grad_pre_rows,
        act_rows,
        cot_rows,
    ) = [jnp.concatenate([item[index] for item in kept_rows], axis=0) for index in range(8)]
    grad_qkv_w = jnp.einsum("td,te->de", h1_rows, grad_qkv_rows, preferred_element_type=jnp.float32)
    grad_out_w = jnp.einsum(
        "td,te->de", attn_rows, grad_after_rows, preferred_element_type=jnp.float32
    )
    attn_matrices = lax.psum_scatter(
        jnp.concatenate([grad_qkv_w, grad_out_w], axis=1),
        ("dp", "ctx"),
        scatter_dimension=0,
        tiled=True,
    )
    grad_fc_w = jnp.einsum("td,tf->df", h2_rows, grad_pre_rows, preferred_element_type=jnp.float32)
    grad_proj_w = jnp.einsum("tf,td->fd", act_rows, cot_rows, preferred_element_type=jnp.float32)
    mlp_matrices = lax.psum_scatter(
        jnp.concatenate(
            [grad_fc_w, grad_proj_w.reshape(lax.axis_size(("dp", "ctx")) * shard_rows, 4 * D)],
            axis=1,
        ),
        ("dp", "ctx"),
        scatter_dimension=0,
        tiled=True,
    )
    column_sums = jnp.sum(grad_qkv_rows, axis=0, dtype=jnp.float32)
    grad_qv_b = jnp.concatenate([column_sums[:D], column_sums[2 * D :]])
    grad_out_b = jnp.sum(grad_after_rows, axis=0, dtype=jnp.float32)
    grad_fc_b = jnp.sum(grad_pre_rows, axis=0, dtype=jnp.float32)
    grad_proj_b = jnp.sum(cot_rows, axis=0, dtype=jnp.float32)
    small_sums = (
        lax.psum_scatter(norm_totals[0], ("dp", "ctx"), scatter_dimension=0, tiled=True),
        lax.psum_scatter(norm_totals[1], ("dp", "ctx"), scatter_dimension=0, tiled=True),
        lax.psum_scatter(grad_qv_b, ("dp", "ctx"), scatter_dimension=0, tiled=True),
        lax.psum_scatter(grad_out_b, ("dp", "ctx"), scatter_dimension=0, tiled=True),
        lax.psum_scatter(norm_totals[2], ("dp", "ctx"), scatter_dimension=0, tiled=True),
        lax.psum_scatter(norm_totals[3], ("dp", "ctx"), scatter_dimension=0, tiled=True),
        lax.psum_scatter(grad_fc_b, ("dp", "ctx"), scatter_dimension=0, tiled=True),
        lax.psum_scatter(grad_proj_b, ("dp", "ctx"), scatter_dimension=0, tiled=True),
    )
    grad_qkv_shard = attn_matrices[:, : 3 * D]
    grad_out_shard = attn_matrices[:, 3 * D :]
    grad_fc_shard = mlp_matrices[:, :FF]
    grad_proj_shard = mlp_matrices[:, FF:].reshape(4 * shard_rows, D)
    summed = (
        lax.psum(small_sums[0].astype(jnp.bfloat16), "rep").astype(jnp.float32),
        lax.psum(small_sums[1].astype(jnp.bfloat16), "rep").astype(jnp.float32),
        lax.psum(grad_qkv_shard.astype(jnp.bfloat16), "rep").astype(jnp.float32),
        lax.psum(small_sums[2].astype(jnp.bfloat16), "rep").astype(jnp.float32),
        lax.psum(grad_out_shard.astype(jnp.bfloat16), "rep").astype(jnp.float32),
        lax.psum(small_sums[3].astype(jnp.bfloat16), "rep").astype(jnp.float32),
        lax.psum(small_sums[4].astype(jnp.bfloat16), "rep").astype(jnp.float32),
        lax.psum(small_sums[5].astype(jnp.bfloat16), "rep").astype(jnp.float32),
        lax.psum(grad_fc_shard.astype(jnp.bfloat16), "rep").astype(jnp.float32),
        lax.psum(small_sums[6].astype(jnp.bfloat16), "rep").astype(jnp.float32),
        lax.psum(grad_proj_shard.astype(jnp.bfloat16), "rep").astype(jnp.float32),
        lax.psum(small_sums[7].astype(jnp.bfloat16), "rep").astype(jnp.float32),
    )
    return (
        jnp.stack(outputs),
        jnp.stack(input_grads),
        summed[0],
        summed[1],
        summed[2],
        summed[3],
        summed[4],
        summed[5],
        summed[6],
        summed[7],
        summed[8],
        summed[9],
        summed[10],
        summed[11],
    )


LANES = 128
SUBLANES = 8
GRANT = 58 << 20
NO_COST = pl.CostEstimate(flops=1, transcendentals=0, bytes_accessed=1)


def permuted(value, axis, pairs):
    if value.ndim < 2 or value.shape[-2] % SUBLANES:
        return lax.ppermute(value, axis, pairs)
    rows = value.reshape(-1, SUBLANES, value.shape[-1])
    return lax.ppermute(rows, axis, pairs).reshape(value.shape)


def over_core(value):
    return permuted(value, "rep", [(0, 1), (1, 0), (2, 3), (3, 2)])


def over_x(value):
    return permuted(value, "rep", [(0, 2), (2, 0), (1, 3), (3, 1)])


def over_y(value):
    return permuted(value, "dp", [(0, 1), (1, 0)])


def ordered(first_is_mine, mine, other):
    return jnp.stack(
        [jnp.where(first_is_mine, mine, other), jnp.where(first_is_mine, other, mine)]
    )


def mxu(left, right, dims=((1,), (0,))):
    return lax.dot_general(left, right, (dims, ((), ())), preferred_element_type=jnp.float32)


def after(value, *others):
    return lax.optimization_barrier((value, *others))[0]


def half_rows(index, core, half):
    mine = (core + index) % 2
    start = 2 * half * index
    return (
        pl.ds(pl.multiple_of(start + half * mine, half), half),
        pl.ds(pl.multiple_of(start + half * (1 - mine), half), half),
    )


def in_sequence(core, valid, mine_ref, other_ref, whole):
    half = mine_ref.shape[0] // CHUNKS
    for index in range(CHUNKS):
        mine, other = half_rows(index, core, half)
        rows = slice(index * half, (index + 1) * half)
        whole[mine, :] = jnp.where(valid, mine_ref[rows, :], 0)
        whole[other, :] = jnp.where(valid, other_ref[rows, :], 0)


def masked_scores(keys, queries, first, count, limit):
    scores = mxu(keys[:count], queries, ((1,), (1,)))
    position = first + lax.broadcasted_iota(jnp.int32, (count - first, queries.shape[0]), 0)
    tail = jnp.where(position < limit, scores[first:], MASKED)
    return tail if first == 0 else jnp.concatenate([scores[:first], tail], axis=0)


def attend_forward_kernel(
    core_ref, limit_ref, q_ref, k_ref, k_other_ref, v_ref, v_other_ref, o_ref, lse_ref, k_all, v_all
):
    pair = pl.program_id(0)
    width = q_ref.shape[0] // 2
    lane = lax.broadcasted_iota(jnp.int32, (1, LANES), 1)
    valid = lane < D - pair * LANES
    queries = jnp.where(valid, q_ref[...], 0) * jnp.asarray(HD ** (-0.5), q_ref.dtype)
    in_sequence(core_ref[0], valid, k_ref, k_other_ref, k_all)
    in_sequence(core_ref[0], valid, v_ref, v_other_ref, v_all)
    keys = k_all[...]
    values_t = v_all[...].T
    for part in range(2):
        rows = slice(part * width, (part + 1) * width)
        first, count = KEY_SPANS[part]
        mixed = []
        for head in range(2):
            own = (lane >= head * HD) & (lane < (head + 1) * HD)
            scores = masked_scores(
                keys, jnp.where(own, queries[rows], 0), first, count, limit_ref[:, rows]
            )
            top = jnp.max(scores, axis=0, keepdims=True)
            expo = jnp.exp(scores - top)
            total = jnp.sum(expo, axis=0, keepdims=True)
            values = values_t[head * HD : (head + 1) * HD, :count]
            mixed.append(mxu(values, expo.astype(jnp.bfloat16)) / total)
            lse_ref[0, head : head + 1, rows] = top + jnp.log(total)
        o_ref[rows, :] = jnp.concatenate(mixed, axis=0).T.astype(o_ref.dtype)


def attend_backward_kernel(
    start,
    core_ref,
    limit_ref,
    q_ref,
    k_ref,
    k_other_ref,
    v_ref,
    v_other_ref,
    grad_ref,
    after_ref,
    lse_ref,
    dq_ref,
    dk_ref,
    dk_other_ref,
    dv_ref,
    dv_other_ref,
    send_a_ref,
    send_b_ref,
    k_all,
    v_all,
    dk_sum,
    dv_sum,
):
    pair = pl.program_id(0) + start
    width = q_ref.shape[0] // 2
    lane = lax.broadcasted_iota(jnp.int32, (1, LANES), 1)
    valid = lane < D - pair * LANES
    queries = jnp.where(valid, q_ref[...], 0) * jnp.asarray(HD ** (-0.5), q_ref.dtype)
    grads = jnp.where(valid, grad_ref[...], 0)
    core = core_ref[0]
    in_sequence(core, valid, k_ref, k_other_ref, k_all)
    in_sequence(core, valid, v_ref, v_other_ref, v_all)
    keys = k_all[...]
    keys_t = keys.T
    values = v_all[...]
    for part in (1, 0):
        rows = slice(part * width, (part + 1) * width)
        first, count = KEY_SPANS[part]
        grad_q, grad_k, grad_v = [], 0.0, 0.0
        for head in range(2):
            own = (lane >= head * HD) & (lane < (head + 1) * HD)
            queries_own = jnp.where(own, queries[rows], 0)
            grads_own = jnp.where(own, grads[rows], 0)
            scores = masked_scores(keys, queries_own, first, count, limit_ref[:, rows])
            probs = jnp.exp(scores - lse_ref[0, head : head + 1, rows])
            grad_probs = mxu(values[:count], grads_own, ((1,), (1,)))
            inner = jnp.sum(probs * grad_probs, axis=0, keepdims=True)
            grad_scores = (probs * (grad_probs - inner)).astype(jnp.bfloat16)
            grad_q.append(mxu(keys_t[head * HD : (head + 1) * HD, :count], grad_scores))
            grad_k += mxu(grad_scores, queries_own)
            grad_v += mxu(probs.astype(jnp.bfloat16), grads_own)
        grad_q = jnp.concatenate(grad_q, axis=0) * HD ** (-0.5)
        dq_ref[rows, :] = grad_q.T.astype(dq_ref.dtype)
        if part == 1:
            dk_sum[...] = grad_k
            dv_sum[...] = grad_v
        else:
            dk_sum[:count, :] += grad_k
            dv_sum[:count, :] += grad_v
    half = dk_ref.shape[0] // CHUNKS
    for index in range(CHUNKS):
        mine, other = half_rows(index, core, half)
        at = slice(index * half, (index + 1) * half)
        dk_ref[at, :] = dk_sum[mine, :].astype(dk_ref.dtype)
        dk_other_ref[at, :] = dk_sum[other, :].astype(dk_ref.dtype)
        dv_ref[at, :] = dv_sum[mine, :].astype(dv_ref.dtype)
        dv_other_ref[at, :] = dv_sum[other, :].astype(dv_ref.dtype)

    @pl.when(core == 0)
    def _():
        send_a_ref[...] = dv_ref[...]
        send_b_ref[...] = after_ref[...]

    @pl.when(core == 1)
    def _():
        send_a_ref[...] = dq_ref[...]
        send_b_ref[...] = dk_ref[...]


CHUNKS = SEQ // PIECE
PAIRS = -(-D // LANES)
GROUPS = ((0, 7), (7, PAIRS))
KEY_SPANS = ((0, 640), (512, 1024))


def by_columns(rows, start=0):
    return pl.BlockSpec((rows, LANES), lambda pair: (0, pair + start))


def attend_forward(core, limit, q, k, k_other, v, v_other):
    rows = q.shape[0]
    return pl.pallas_call(
        attend_forward_kernel,
        grid=(PAIRS,),
        in_specs=[
            pl.BlockSpec(memory_space=pltpu.SMEM),
            pl.BlockSpec((1, rows), lambda pair: (0, 0)),
        ]
        + [by_columns(rows)] * 5,
        out_specs=[by_columns(rows), pl.BlockSpec((1, 2, rows), lambda pair: (pair, 0, 0))],
        out_shape=[
            jax.ShapeDtypeStruct((rows, D), jnp.bfloat16),
            jax.ShapeDtypeStruct((PAIRS, 2, rows), jnp.float32),
        ],
        scratch_shapes=[pltpu.VMEM((2 * rows, LANES), jnp.bfloat16)] * 2,
        cost_estimate=NO_COST,
        compiler_params=pltpu.CompilerParams(vmem_limit_bytes=GRANT),
        name="attend_forward",
    )(core, limit, q, k, k_other, v, v_other)


def attend_backward(group, core, limit, q, k, k_other, v, v_other, grad, grad_after, lse):
    rows = q.shape[0]
    start, stop = group
    columns = min(D, stop * LANES) - start * LANES
    return pl.pallas_call(
        lambda *refs: attend_backward_kernel(start, *refs),
        grid=(stop - start,),
        in_specs=[
            pl.BlockSpec(memory_space=pltpu.SMEM),
            pl.BlockSpec((1, rows), lambda pair: (0, 0)),
        ]
        + [by_columns(rows, start)] * 7
        + [pl.BlockSpec((1, 2, rows), lambda pair: (pair + start, 0, 0))],
        out_specs=[by_columns(rows)] * 7,
        out_shape=[jax.ShapeDtypeStruct((rows, columns), jnp.bfloat16)] * 7,
        scratch_shapes=[pltpu.VMEM((2 * rows, LANES), jnp.bfloat16)] * 2
        + [pltpu.VMEM((2 * rows, LANES), jnp.float32)] * 2,
        cost_estimate=NO_COST,
        compiler_params=pltpu.CompilerParams(vmem_limit_bytes=GRANT),
        name="attend_backward",
    )(core, limit, q, k, k_other, v, v_other, grad, grad_after, lse)


def weight_gradient_kernel(count, place_ref, *refs):
    lefts, rights = list(refs[:count]), list(refs[count:-3])
    send_ref, keep_ref, whole = refs[-3:]
    block = lefts[0].shape[1]
    total, left_at, right_at = 0.0, 0, 0
    while lefts:
        rows = min(lefts[0].shape[0] - left_at, rights[0].shape[0] - right_at)
        left = lefts[0][left_at : left_at + rows, :]
        total += mxu(left, rights[0][right_at : right_at + rows, :], ((0,), (0,)))
        left_at, right_at = left_at + rows, right_at + rows
        if left_at == lefts[0].shape[0]:
            lefts, left_at = lefts[1:], 0
        if right_at == rights[0].shape[0]:
            rights, right_at = rights[1:], 0
    step = pl.program_id(0)
    whole[pl.ds(pl.multiple_of(step * block, block), block), :] = total.astype(whole.dtype)

    @pl.when(step == pl.num_programs(0) - 1)
    def _():
        rows, dp = send_ref.shape[0], place_ref[1]
        send_ref[...] = whole[pl.ds(pl.multiple_of((1 - dp) * rows, rows), rows), :]
        keep_ref[...] = whole[pl.ds(pl.multiple_of(dp * rows, rows), rows), :]


def weight_gradient(place, lefts, rights, block=256):
    inner, outer = lefts[0].shape[1], rights[0].shape[1]
    steps = pl.cdiv(inner, block)
    return pl.pallas_call(
        lambda *refs: weight_gradient_kernel(len(lefts), *refs),
        grid=(steps,),
        in_specs=[pl.BlockSpec(memory_space=pltpu.SMEM)]
        + [pl.BlockSpec((left.shape[0], block), lambda i: (0, i)) for left in lefts]
        + [
            pl.BlockSpec(right.shape, lambda i: (0, 0), pipeline_mode=pl.Buffered(1))
            for right in rights
        ],
        out_specs=[pl.BlockSpec((inner // 2, outer), lambda i: (0, 0))] * 2,
        out_shape=[jax.ShapeDtypeStruct((inner // 2, outer), jnp.bfloat16)] * 2,
        scratch_shapes=[pltpu.VMEM((steps * block, outer), jnp.bfloat16)],
        cost_estimate=NO_COST,
        compiler_params=pltpu.CompilerParams(vmem_limit_bytes=GRANT),
        name="weight_gradient",
    )(place, *lefts, *rights)


def pair_sum_kernel(first_ref, second_ref, out_ref):
    total = first_ref[...].astype(jnp.float32) + second_ref[...].astype(jnp.float32)
    out_ref[...] = total.astype(out_ref.dtype)


def pair_sum(first, second, block=200):
    spec = pl.BlockSpec((block, first.shape[1]), lambda i: (i, 0))
    return pl.pallas_call(
        pair_sum_kernel,
        grid=(first.shape[0] // block,),
        in_specs=[spec, spec],
        out_specs=spec,
        out_shape=jax.ShapeDtypeStruct(first.shape, first.dtype),
        cost_estimate=NO_COST,
        compiler_params=pltpu.CompilerParams(vmem_limit_bytes=GRANT),
        name="pair_sum",
    )(first, second)


def second_terms_kernel(place_ref, *refs):
    came_x, came_y, kept_x, kept_y, send_x, send_y, stay_x, stay_y = refs
    dp, chip_x = place_ref[1], place_ref[0] // 2
    f32 = jnp.float32
    for kept, came, own, send, stay in (
        (kept_x, came_x, dp, send_x, stay_x),
        (kept_y, came_y, chip_x, send_y, stay_y),
    ):
        send[...] = (kept[1 - own].astype(f32) + came[1 - own].astype(f32)).astype(send.dtype)
        stay[...] = (kept[own].astype(f32) + came[own].astype(f32)).astype(send.dtype)


def second_terms(place, came_x, came_y, kept_x, kept_y):
    shape = jax.ShapeDtypeStruct(came_x.shape[1:], came_x.dtype)
    return pl.pallas_call(
        second_terms_kernel,
        in_specs=[pl.BlockSpec(memory_space=pltpu.SMEM)]
        + [pl.BlockSpec(memory_space=pltpu.VMEM)] * 4,
        out_specs=[pl.BlockSpec(memory_space=pltpu.VMEM)] * 4,
        out_shape=[shape] * 4,
        cost_estimate=NO_COST,
        compiler_params=pltpu.CompilerParams(vmem_limit_bytes=GRANT),
        name="second_terms",
    )(place, came_x, came_y, kept_x, kept_y)


def summed_kernel(came_x, came_y, stay_x, stay_y, out_ref):
    rows = stay_x.shape[0]
    f32 = jnp.float32
    out_ref[:rows, :] = (stay_x[...].astype(f32) + came_x[...].astype(f32)).astype(out_ref.dtype)
    out_ref[rows:, :] = (stay_y[...].astype(f32) + came_y[...].astype(f32)).astype(out_ref.dtype)


def summed(came_x, came_y, stay_x, stay_y):
    rows, width = stay_x.shape
    return pl.pallas_call(
        summed_kernel,
        in_specs=[pl.BlockSpec(memory_space=pltpu.VMEM)] * 4,
        out_specs=pl.BlockSpec(memory_space=pltpu.VMEM),
        out_shape=jax.ShapeDtypeStruct((2 * rows, width), stay_x.dtype),
        cost_estimate=NO_COST,
        compiler_params=pltpu.CompilerParams(vmem_limit_bytes=GRANT),
        name="summed",
    )(came_x, came_y, stay_x, stay_y)


def block_value_kernel(after_ref, own_ref, core_ref, far_ref, bias_ref, out_ref):
    f32 = jnp.float32
    value = after_ref[...] + own_ref[...].astype(f32) + core_ref[...].astype(f32)
    out_ref[...] = (value + far_ref[...].astype(f32) + bias_ref[...]).astype(out_ref.dtype)


def block_value_of(after_attn, own, core, far, bias, block=128):
    spec = pl.BlockSpec((block, D), lambda i: (i, 0))
    return pl.pallas_call(
        block_value_kernel,
        grid=(own.shape[0] // block,),
        in_specs=[spec] * 4 + [pl.BlockSpec((1, D), lambda i: (0, 0))],
        out_specs=spec,
        out_shape=jax.ShapeDtypeStruct(own.shape, jnp.bfloat16),
        cost_estimate=NO_COST,
        compiler_params=pltpu.CompilerParams(vmem_limit_bytes=GRANT),
        name="block_value",
    )(after_attn, own, core, far, bias)


def attention_weights_kernel(
    place_ref,
    hidden_ref,
    hidden_other_ref,
    left_ref,
    left_other_ref,
    dq_ref,
    dk_ref,
    dk_other_ref,
    dv_ref,
    dv_other_ref,
    after_ref,
    key_came_ref,
    value_came_ref,
    came_a_ref,
    came_b_ref,
    send_x_ref,
    keep_x_ref,
    send_y_ref,
    keep_y_ref,
    right,
    terms,
):
    rep, dp = place_ref[0], place_ref[1]
    chip_x, core = rep // 2, rep % 2
    rows, width = dq_ref.shape
    low, f32 = jnp.bfloat16, jnp.float32
    own, other = slice(0, rows), slice(rows, 2 * rows)
    add = lambda first, second: (first[...].astype(f32) + second[...].astype(f32)).astype(low)

    @pl.when(core == 0)
    def _():
        right[0, own, :] = dq_ref[...]
        right[0, other, :] = came_a_ref[...]
        right[1, own, :] = add(dk_ref, key_came_ref)
        right[1, other, :] = add(dk_other_ref, came_b_ref)

    @pl.when(core == 1)
    def _():
        right[0, own, :] = add(dv_ref, value_came_ref)
        right[0, other, :] = add(dv_other_ref, came_a_ref)
        right[1, own, :] = after_ref[:, :width]
        right[1, other, :] = came_b_ref[...]

    for index, lefts in enumerate(((hidden_ref, hidden_other_ref), (left_ref, left_other_ref))):
        for at in range(0, D, 256):
            columns = slice(at, min(D, at + 256))
            term = mxu(lefts[0][:, columns], right[index, own, :], ((0,), (0,)))
            term += mxu(lefts[1][:, columns], right[index, other, :], ((0,), (0,)))
            terms[index, columns, :] = term.astype(low)
    quarter = D // 4
    for side in range(2):
        part = pl.ds(2 * side * quarter, quarter)
        send_x_ref[side] = terms[1 - chip_x, part, :]
        keep_x_ref[side] = terms[chip_x, part, :]
    for index in range(2):
        start = lambda at: pl.ds(pl.multiple_of((2 * at + 1) * quarter, quarter), quarter)
        send_y_ref[index] = terms[index, start(1 - dp), :]
        keep_y_ref[index] = terms[index, start(dp), :]


def attention_weights(place, hidden, hidden_other, left, left_other, grads, came):
    rows, width = grads[0].shape
    shape = jax.ShapeDtypeStruct((2, D // 4, width), jnp.bfloat16)
    arrays = [hidden, hidden_other, left, left_other, *grads, *came]
    return pl.pallas_call(
        attention_weights_kernel,
        in_specs=[pl.BlockSpec(memory_space=pltpu.SMEM)]
        + [pl.BlockSpec(memory_space=pltpu.VMEM)] * len(arrays),
        out_specs=[pl.BlockSpec(memory_space=pltpu.VMEM)] * 4,
        out_shape=[shape] * 4,
        scratch_shapes=[
            pltpu.VMEM((2, 2 * rows, width), jnp.bfloat16),
            pltpu.VMEM((2, D, width), jnp.bfloat16),
        ],
        cost_estimate=NO_COST,
        compiler_params=pltpu.CompilerParams(vmem_limit_bytes=GRANT),
        name="attention_weights",
    )(place, *arrays)


QUERY, VALUE, KEY, OUT = range(4)


def matrix_copies(place_ref, role, pieces, whole, sems):
    rep, dp = place_ref[0], place_ref[1]
    count = pieces[0].shape[0]
    copies = []
    for t in range(4):
        copies.append([])
        for side in range(2):
            start = pl.multiple_of((dp if side == 0 else 1 - dp) * count, count)
            copies[t].append(
                pltpu.make_async_copy(
                    pieces[2 * t + side], whole.at[pl.ds(start, count), :], sems.at[side]
                )
            )

    def start():
        for t in range(4):

            @pl.when((rep ^ t) == role)
            def _():
                copies[t][0].start()
                copies[t][1].start()

    def wait():
        copies[0][0].wait()
        copies[0][1].wait()

    return start, wait


def row_norm(values):
    center = values - jnp.mean(values, axis=-1, keepdims=True)
    inv_std = lax.rsqrt(jnp.mean(center * center, axis=-1, keepdims=True) + EPSILON)
    return center * inv_std, inv_std


def row_norm_back(upstream, normed, inv_std, gain):
    scaled = upstream * gain
    inner = (
        scaled
        - jnp.mean(scaled, axis=-1, keepdims=True)
        - normed * jnp.mean(scaled * normed, axis=-1, keepdims=True)
    )
    return inner * inv_std


def column_sum(values):
    return jnp.sum(values, axis=0, keepdims=True)


STRIP = 128


def strips(ref):
    return [slice(at, at + STRIP) for at in range(0, ref.shape[0], STRIP)]


def project_kernel(place_ref, tokens_ref, gain_ref, shift_ref, bias_ref, *refs):
    pieces, (h_ref, q_ref, k_ref, v_ref, weights, sems) = refs[:8], refs[8:]
    loads = [
        matrix_copies(place_ref, role, pieces, weights.at[slot], sems.at[slot])
        for slot, role in enumerate((QUERY, VALUE, KEY))
    ]
    for start, _ in loads:
        start()
    for rows in strips(tokens_ref):
        normed, _ = row_norm(tokens_ref[rows, :].astype(jnp.float32))
        h_ref[rows, :] = (normed * gain_ref[...] + shift_ref[...]).astype(h_ref.dtype)
    hidden = h_ref[...]
    loads[0][1]()
    q_ref[...] = (mxu(hidden, weights[0]) + bias_ref[:, :D]).astype(q_ref.dtype)
    loads[1][1]()
    v_ref[...] = (mxu(hidden, weights[1]) + bias_ref[:, D:]).astype(v_ref.dtype)
    loads[2][1]()
    k_ref[...] = mxu(hidden, weights[2]).astype(k_ref.dtype)


def out_kernel(place_ref, attn_ref, hidden_ref, tokens_ref, bias_ref, gain_ref, shift_ref, *refs):
    pieces, (x_ref, h_ref, left_ref, send_ref, weight, sems) = refs[:8], refs[8:]
    start, wait = matrix_copies(place_ref, OUT, pieces, weight, sems)
    start()
    low_core = place_ref[0] % 2 == 0
    left_ref[...] = jnp.where(low_core, hidden_ref[...], attn_ref[...])
    send_ref[...] = jnp.where(low_core, attn_ref[...], hidden_ref[...])
    wait()
    x_ref[...] = mxu(attn_ref[...], weight[...])
    for rows in strips(x_ref):
        value = tokens_ref[rows, :].astype(jnp.float32) + x_ref[rows, :] + bias_ref[...]
        x_ref[rows, :] = value
        normed, _ = row_norm(value)
        h_ref[rows, :] = (normed * gain_ref[...] + shift_ref[...]).astype(h_ref.dtype)


def out_back_kernel(place_ref, own_ref, core_ref, far_ref, x_ref, cot_ref, gain_ref, *refs):
    pieces, (after_ref, low_ref, grad_ref, sum_ref, weight, sems) = refs[:8], refs[8:]
    start, wait = matrix_copies(place_ref, OUT, pieces, weight, sems)
    start()
    f32 = jnp.float32
    totals = [0.0] * 4
    for rows in strips(x_ref):
        grad_h = own_ref[rows, :].astype(f32) + core_ref[rows, :].astype(f32)
        grad_h += far_ref[rows, :].astype(f32)
        normed, inv_std = row_norm(x_ref[rows, :])
        value = row_norm_back(grad_h, normed, inv_std, gain_ref[...]) + cot_ref[rows, :].astype(f32)
        after_ref[rows, :] = value
        value_low = value.astype(low_ref.dtype)
        low_ref[rows, :] = value_low
        terms = (grad_h * normed, grad_h, value_low.astype(f32), cot_ref[rows, :].astype(f32))
        totals = [total + column_sum(term) for total, term in zip(totals, terms)]
    for index, total in enumerate(totals):
        sum_ref[index : index + 1, :] = total
    wait()
    grad_ref[...] = mxu(low_ref[...], weight[...], ((1,), (1,))).astype(grad_ref.dtype)


def project_back_kernel(groups, place_ref, tokens_ref, after_ref, gain_ref, *refs):
    count = 5 * len(groups)
    grads, pieces = refs[:count], refs[count : count + 8]
    out_ref, sum_ref, weights, grad_h, sems = refs[count + 8 :]
    f32 = jnp.float32
    loads = [
        matrix_copies(place_ref, role, pieces, weights.at[slot], sems.at[slot])
        for slot, role in enumerate((QUERY, VALUE, KEY))
    ]
    for start, _ in loads:
        start()
    for slot in range(3):
        loads[slot][1]()
        for index, columns in enumerate(groups):
            query, value, value_came, key, key_came = grads[5 * index : 5 * index + 5]
            if slot == 0:
                grad = query[...]
            else:
                near, came = (value, value_came) if slot == 1 else (key, key_came)
                grad = (near[...].astype(f32) + came[...].astype(f32)).astype(query.dtype)
            term = mxu(grad, weights[slot, :, columns], ((1,), (1,)))
            if slot == 0 and index == 0:
                grad_h[...] = term
            else:
                grad_h[...] += term
            if slot < 2:
                sum_ref[2 + slot : 3 + slot, columns] = column_sum(grad.astype(f32))
    totals = [0.0, 0.0]
    for rows in strips(tokens_ref):
        upstream = grad_h[rows, :]
        normed, inv_std = row_norm(tokens_ref[rows, :].astype(f32))
        value = row_norm_back(upstream, normed, inv_std, gain_ref[...]) + after_ref[rows, :]
        out_ref[rows, :] = value.astype(out_ref.dtype)
        terms = (upstream * normed, upstream)
        totals = [total + column_sum(term) for total, term in zip(totals, terms)]
    for index, total in enumerate(totals):
        sum_ref[index : index + 1, :] = total


def on_chip(body, name, place, arrays, pieces, outs, scratch):
    return pl.pallas_call(
        body,
        in_specs=[pl.BlockSpec(memory_space=pltpu.SMEM)]
        + [pl.BlockSpec(memory_space=pltpu.VMEM)] * len(arrays)
        + [pl.BlockSpec(memory_space=pl.ANY)] * len(pieces),
        out_specs=[pl.BlockSpec(memory_space=pltpu.VMEM)] * len(outs),
        out_shape=[jax.ShapeDtypeStruct(*out) for out in outs],
        scratch_shapes=scratch,
        cost_estimate=NO_COST,
        compiler_params=pltpu.CompilerParams(vmem_limit_bytes=GRANT),
        name=name,
    )(place, *arrays, *pieces)


def feed_forward_kernel(place_ref, *refs):
    h_ref, h_core_ref, cot_ref, cot_core_ref, bias_ref, *refs = refs
    pieces, refs = refs[:4], refs[4:]
    act_ref, pre_ref, out_ref, out_core_ref, back_ref, back_core_ref, sum_ref, fc, proj, sems = refs
    step = pl.program_id(0)
    dp = place_ref[1]

    @pl.when(step == 0)
    def _():
        copies = []
        for index, piece in enumerate(pieces):
            whole = fc if index < 2 else proj
            count = piece.shape[0]
            start = pl.multiple_of((dp if index % 2 == 0 else 1 - dp) * count, count)
            copies.append(
                pltpu.make_async_copy(piece, whole.at[pl.ds(start, count), :], sems.at[index])
            )
        for copy in copies:
            copy.start()
        for copy in copies:
            copy.wait()
        sum_ref[...] = jnp.zeros_like(sum_ref)

    own = step < pl.num_programs(0) // 2
    hidden = jnp.where(own, h_ref[...], h_core_ref[...])
    cotangent = jnp.where(own, cot_ref[...], cot_core_ref[...])
    hidden_act, hidden_slope = gelu_both(mxu(hidden, fc[...]) + bias_ref[...])
    act_low = hidden_act.astype(jnp.bfloat16)
    act_ref[...] = act_low
    out = mxu(act_low, proj[...]).astype(out_ref.dtype)
    grad_act = mxu(cotangent, proj[...], ((1,), (1,)))
    pre_low = (grad_act * hidden_slope).astype(jnp.bfloat16)
    pre_ref[...] = pre_low
    back = mxu(pre_low, fc[...], ((1,), (1,))).astype(back_ref.dtype)
    sum_ref[...] += column_sum(pre_low.astype(jnp.float32))

    @pl.when(own)
    def _():
        out_ref[...] = out
        back_ref[...] = back

    @pl.when(jnp.logical_not(own))
    def _():
        out_core_ref[...] = out
        back_core_ref[...] = back


def feed_forward(place, hidden, hidden_core, cot, cot_core, bias, pieces, block_rows=256):
    rows, units = hidden.shape[0], D
    steps = rows // block_rows
    first = pl.BlockSpec((block_rows, D), lambda i: (jnp.minimum(i, steps - 1), 0))
    second = pl.BlockSpec((block_rows, D), lambda i: (jnp.maximum(i - steps, 0), 0))
    by_block = pl.BlockSpec((block_rows, D), lambda i: (i, 0))
    return pl.pallas_call(
        feed_forward_kernel,
        grid=(2 * steps,),
        in_specs=[pl.BlockSpec(memory_space=pltpu.SMEM), first, second, first, second]
        + [pl.BlockSpec((1, units), lambda i: (0, 0))]
        + [pl.BlockSpec(memory_space=pl.ANY)] * 4,
        out_specs=[by_block, by_block, first, second, first, second]
        + [pl.BlockSpec((1, units), lambda i: (0, 0))],
        out_shape=[jax.ShapeDtypeStruct((2 * rows, D), jnp.bfloat16)] * 2
        + [jax.ShapeDtypeStruct((rows, D), jnp.bfloat16)] * 4
        + [jax.ShapeDtypeStruct((1, units), jnp.float32)],
        scratch_shapes=[pltpu.VMEM((D, D), jnp.bfloat16)] * 2 + [pltpu.SemaphoreType.DMA((4,))],
        cost_estimate=NO_COST,
        compiler_params=pltpu.CompilerParams(vmem_limit_bytes=GRANT),
        name="feed_forward",
    )(place, hidden, hidden_core, cot, cot_core, bias, *pieces)


def unpack_kernel(widths, rep_ref, small_ref, *out_refs):
    chips, count, _ = small_ref.shape
    shards = chips * count
    at = 0
    for width, out_ref in zip(widths, out_refs):
        pieces = [
            small_ref[shard % chips, shard // chips : shard // chips + 1, at : at + width]
            for shard in range(shards)
        ]
        at += width
        if width * shards == out_ref.shape[1]:
            out_ref[...] = jnp.concatenate(pieces, axis=1).astype(jnp.float32)
            continue
        part = width // 4
        for rep in range(4):

            @pl.when(rep_ref[0] == rep)
            def _():
                own = [piece[:, rep * part : (rep + 1) * part] for piece in pieces]
                out_ref[...] = jnp.concatenate(own, axis=1).astype(jnp.float32)


def unpack(rep, small, widths, picked):
    shards = small.shape[0] * small.shape[1]
    return pl.pallas_call(
        lambda *refs: unpack_kernel(widths, *refs),
        in_specs=[
            pl.BlockSpec(memory_space=pltpu.SMEM),
            pl.BlockSpec(memory_space=pltpu.VMEM),
        ],
        out_specs=[pl.BlockSpec(memory_space=pltpu.VMEM)] * len(widths),
        out_shape=[
            jax.ShapeDtypeStruct((1, width * shards // (4 if index == picked else 1)), jnp.float32)
            for index, width in enumerate(widths)
        ],
        cost_estimate=NO_COST,
        compiler_params=pltpu.CompilerParams(vmem_limit_bytes=GRANT),
        name="unpack",
    )(rep.astype(jnp.int32)[None], small)


def pick_kernel(rep_ref, whole_ref, part_ref):
    count = part_ref.shape[0]
    for rep in range(4):

        @pl.when(rep_ref[0] == rep)
        def _():
            pieces = [
                whole_ref[:, at : at + count] for at in range(rep * count, whole_ref.shape[1], 4 * count)
            ]
            part_ref[...] = jnp.concatenate(pieces, axis=1)


def pick_units(rep, whole):
    return pl.pallas_call(
        pick_kernel,
        in_specs=[
            pl.BlockSpec(memory_space=pltpu.SMEM),
            pl.BlockSpec(memory_space=pltpu.VMEM),
        ],
        out_specs=pl.BlockSpec(memory_space=pltpu.VMEM),
        out_shape=jax.ShapeDtypeStruct((whole.shape[0], whole.shape[1] // 4), whole.dtype),
        compiler_params=pltpu.CompilerParams(vmem_limit_bytes=GRANT),
        name="pick_units",
    )(rep.astype(jnp.int32)[None], whole)


def merge_kernel(parts_ref, whole_ref):
    count = parts_ref.shape[1]
    for at in range(0, parts_ref.shape[2], count):
        pieces = [parts_ref[core * 2 + x, :, at : at + count] for x in range(2) for core in range(2)]
        whole_ref[:, 4 * at : 4 * (at + count)] = jnp.concatenate(pieces, axis=1).astype(whole_ref.dtype)


def merge_units(parts):
    return pl.pallas_call(
        merge_kernel,
        in_specs=[pl.BlockSpec(memory_space=pltpu.VMEM)],
        out_specs=pl.BlockSpec(memory_space=pltpu.VMEM),
        out_shape=jax.ShapeDtypeStruct((parts.shape[1], 4 * parts.shape[2]), jnp.float32),
        compiler_params=pltpu.CompilerParams(vmem_limit_bytes=GRANT),
        name="merge_units",
    )(parts)


def sequence_local(
    hidden_in,
    piece_starts,
    grad_out,
    attn_gain,
    attn_shift,
    qkv_weight,
    qv_bias,
    out_weight,
    out_bias,
    mlp_gain,
    mlp_shift,
    fc_weight,
    fc_bias,
    proj_weight,
    proj_bias,
):
    rep, dp, ctx = (lax.axis_index(name) for name in ("rep", "dp", "ctx"))
    chip_x, core = rep // 2, rep % 2
    chips, shards = lax.axis_size("ctx"), lax.axis_size(("dp", "ctx"))
    seqs, block, _ = hidden_in.shape
    half = block // 2
    rows = chips * half
    shard_rows = D // shards
    f32, low = jnp.float32, jnp.bfloat16
    core_low, x_low, y_low = core == 0, chip_x == 0, dp == 0
    half_of = lambda index: (core + index) % 2

    def exchange(tiles):
        return lax.all_to_all(tiles, "ctx", 0, 0, tiled=True)

    def tiled(value):
        return value.reshape(chips, half // SUBLANES, SUBLANES, D)

    def by_sequence(value):
        halves = value.reshape(seqs, 2, half // SUBLANES, SUBLANES, D)
        mine = half_of(ctx)
        kept = lax.dynamic_index_in_dim(halves, mine, 1, keepdims=False)
        came = over_core(lax.dynamic_index_in_dim(halves, 1 - mine, 1, keepdims=False))
        return tiled(ordered(core_low, kept, came))

    def from_sequence(every):
        every = every.reshape(2, seqs, half // SUBLANES, SUBLANES, D)
        kept = lax.dynamic_index_in_dim(every, core, 0, keepdims=False)
        came = over_core(lax.dynamic_index_in_dim(every, 1 - core, 0, keepdims=False))
        both = ordered(half_of(ctx) == 0, kept, came)
        return both.transpose(1, 0, 2, 3, 4).reshape(seqs, block, D)

    def along_ctx(shard):
        return lax.all_gather(shard, "ctx", axis=0, tiled=True)

    items = (attn_gain, attn_shift, qv_bias, out_bias, mlp_gain, mlp_shift, fc_bias, proj_bias)
    small = jnp.concatenate(items)[None]
    small = ordered(y_low, small, over_y(small)).reshape(1, 2, -1)
    small = lax.all_to_all(
        jnp.broadcast_to(small, (chips,) + small.shape[1:]), "ctx", 0, 0, tiled=True
    )

    shard_attn = jnp.where(
        x_low,
        jnp.where(core_low, qkv_weight[:, :D], qkv_weight[:, 2 * D :]),
        jnp.where(core_low, qkv_weight[:, D : 2 * D], out_weight),
    )
    shard_fc = pick_units(rep, fc_weight)
    shard_proj = lax.dynamic_index_in_dim(
        proj_weight.reshape(4, shard_rows, D), rep, 0, keepdims=False
    )
    mine = along_ctx(shard_attn)
    tokens_sent = by_sequence(after(hidden_in, shard_attn))
    cot_sent = by_sequence(after(grad_out, tokens_sent))
    tokens_low = exchange(tokens_sent).reshape(rows, D)
    mine_fc = along_ctx(shard_fc)
    mine_proj = along_ctx(shard_proj)

    every_starts = ordered(core_low, piece_starts, over_core(piece_starts)).reshape(chips, -1)
    starts = lax.dynamic_index_in_dim(every_starts, ctx, 0, keepdims=False)
    block_index = jnp.arange(chips)
    row_pos = (
        (block_index * block + half_of(block_index) * half)[:, None] + jnp.arange(half)[None, :]
    ).reshape(rows)
    inside = (row_pos[:, None] >= starts[None, :]) & (row_pos[:, None] < starts[None, :] + PIECE)
    limit = jnp.maximum(row_pos + 1, jnp.max(jnp.where(inside, starts[None, :] + PIECE, 0), axis=1))
    limit = limit.astype(jnp.int32)[None, :]
    core_id = core.astype(jnp.int32)[None]

    place = jnp.stack([rep, dp]).astype(jnp.int32)

    vectors = unpack(rep, small, [item.shape[0] for item in items], 6)
    mine, vectors = lax.optimization_barrier(
        (mine, vectors, shard_fc, shard_proj, tokens_low, cot_sent, limit)
    )[:2]
    gain_one, shift_one, qv_full, out_bias_full, gain_two, shift_two, fc_bias_mine, proj_bias_full = vectors
    other, mine_x = lax.optimization_barrier((over_y(mine), over_x(mine)))
    cot_low = exchange(after(cot_sent, mine_fc)).reshape(rows, D)
    other_x, cot_low, fc_other = lax.optimization_barrier((over_x(other), cot_low, over_y(mine_fc)))
    pieces = []
    for pair in ((mine, other), (mine_x, other_x)):
        pieces += [pair[0], pair[1], over_core(pair[0]), over_core(pair[1])]

    h1_low, query_low, key_low, value_low = on_chip(
        project_kernel,
        "project",
        place,
        [tokens_low] + [gain_one, shift_one, qv_full],
        pieces,
        [((rows, D), low)] * 4,
        [pltpu.VMEM((3, D, D), low), pltpu.SemaphoreType.DMA((3, 2))],
    )
    key_other, value_other = over_core(key_low), over_core(value_low)
    proj_other = over_y(mine_proj)
    query_low = after(query_low, mine_proj)
    attn_low, lse = attend_forward(
        core_id, limit, query_low, key_low, key_other, value_low, value_other
    )
    cot_x, cot_core = over_x(cot_low), over_core(cot_low)
    after_attn, h2_low, left_b, send_b = on_chip(
        out_kernel,
        "attention_out",
        place,
        [after(attn_low, cot_x, proj_other), h1_low, tokens_low, out_bias_full, gain_two, shift_two],
        pieces,
        [((rows, D), f32)] + [((rows, D), low)] * 3,
        [pltpu.VMEM((D, D), low), pltpu.SemaphoreType.DMA((2,))],
    )

    h2_x, h2_core = over_x(h2_low), over_core(h2_low)
    proj_other = after(proj_other, h2_core)
    pieces_fc = [mine_fc, fc_other, mine_proj, proj_other]
    act_near, pre_near, out_near, out_core, back_near, back_core, sum_near = feed_forward(
        place, h2_low, h2_core, cot_low, cot_core, fc_bias_mine, pieces_fc
    )
    cot_x = after(cot_x, back_near)
    h2_x = after(h2_x, cot_x)
    cot_xc, h2_xc = over_core(cot_x), over_core(h2_x)
    act_far, pre_far, out_x, out_xc, back_x, back_xc, sum_far = feed_forward(
        place, h2_x, h2_xc, cot_x, cot_xc, fc_bias_mine, pieces_fc
    )

    def far_sum(own, core):
        return pair_sum(own, over_core(core), 128)

    back_x = far_sum(back_x, back_xc)
    back_came = over_x(back_x)
    back_core = over_core(back_core)
    out_x = far_sum(out_x, out_xc)
    act_near, pre_near = after((act_near, pre_near), back_x, out_x, back_core)
    proj_send, proj_kept = weight_gradient(
        place, [act_near, act_far], [cot_low, cot_core, cot_x, cot_xc])
    back_came = after(back_came, proj_send)
    out_came, out_core = over_x(after(out_x, back_came)), over_core(out_core)
    grad_after, grad_after_low, grad_attn_low, sums_two = on_chip(
        out_back_kernel,
        "attention_out_back",
        place,
        [back_near, back_core, back_came, after_attn, cot_low, gain_two],
        pieces,
        [((rows, D), f32), ((rows, D), low), ((rows, D), low), ((4, D), f32)],
        [pltpu.VMEM((D, D), low), pltpu.SemaphoreType.DMA((2,))],
    )

    proj_came = over_y(after(proj_send, back_came))

    def finish(value):
        return lax.psum_scatter(value, "ctx", scatter_dimension=0, tiled=True)

    def share(value):
        pair = ordered(x_low, value, over_x(value))
        return ordered(core_low, pair, over_core(pair)).reshape((4,) + value.shape)

    h1_other, left_b_other = over_core(h1_low), over_core(send_b)

    grads, terms = [], []
    held, spans = (), []
    for group in GROUPS:
        columns = slice(group[0] * LANES, min(D, group[1] * LANES))
        spans.append(columns)
        dq, dk, dk_other, dv, dv_other, send_one, send_two = attend_backward(
            group,
            core_id,
            limit,
            query_low,
            key_low,
            key_other,
            value_low,
            value_other,
            after(grad_attn_low, *held),
            grad_after_low,
            lse,
        )
        crossing = (dk_other, dv_other, send_one, send_two)
        came = [over_core(item) for item in crossing]
        if not group[0]:
            pre_near = after(pre_near, dq, out_came)
            fc_send, fc_kept = weight_gradient(
                place, [h2_low, h2_core, h2_x, h2_xc], [pre_near, pre_far]
            )
            fc_came = over_y(fc_send)
            proj_total = pair_sum(proj_kept, after(proj_came, fc_send))
            proj_sum = finish(proj_total)
            h1_low = after(h1_low, proj_total)
        else:
            fc_total = pair_sum(fc_kept, after(fc_came, dq))
            fc_sum = finish(fc_total)
            h1_low = after(h1_low, fc_total)
        send_x, keep_x, send_y, keep_y = attention_weights(
            place,
            h1_low,
            h1_other,
            left_b,
            left_b_other,
            [dq, dk, dk_other, dv, dv_other, grad_after_low[:, columns]],
            came,
        )
        terms.append((over_x(send_x), over_y(send_y), keep_x, keep_y))
        held = (keep_x,)
        grads.append((dq, dv, came[1], dk, came[0]))
        if not group[0]:
            out_came = after(out_came, keep_x)
            block_tiles = tiled(block_value_of(after_attn, out_near, out_core, out_came, proj_bias_full))
            block_sent = exchange(block_tiles)
    came = after(terms[0][:2], *held)
    second_0 = second_terms(place, *came, *terms[0][2:])
    grad_input_low, sums_one = on_chip(
        lambda *refs: project_back_kernel(spans, *refs),
        "project_back",
        place,
        [tokens_low, after(grad_after, *held, block_tiles, *second_0), gain_one] + [item for group in grads for item in group],
        pieces,
        [((rows, D), low), ((4, D), f32)],
        [
            pltpu.VMEM((3, D, D), low),
            pltpu.VMEM((rows, D), f32),
            pltpu.SemaphoreType.DMA((3, 2)),
        ],
    )
    came = after((over_y(second_0[0]), over_x(second_0[1])), grad_input_low, block_sent)
    total_0 = summed(*came, *second_0[2:])
    sum_0 = finish(total_0)
    input_sent = exchange(tiled(after(grad_input_low, total_0)))
    came = after(terms[1][:2], total_0)
    second_1 = second_terms(place, *came, *terms[1][2:])
    proj_quarters = share(after(proj_sum, *second_1))
    came = after((over_y(second_1[0]), over_x(second_1[1])), proj_quarters)
    total_1 = summed(*came, *second_1[2:])
    sum_1 = finish(total_1)
    block_out = from_sequence(after(block_sent, total_1))
    fc_quarters = share(after(fc_sum, block_out))
    grad_fc_shard = merge_units(fc_quarters)
    grad_proj_shard = (
        proj_quarters.reshape(2, 2, shard_rows, D)
        .transpose(1, 0, 2, 3)
        .reshape(4 * shard_rows, D)
        .astype(f32)
    )
    share_0 = share(after(sum_0, fc_quarters))
    input_grad = from_sequence(after(input_sent, share_0)).astype(f32)
    sum_1 = after(sum_1, input_grad, grad_fc_shard, grad_proj_shard)
    share_1 = share(sum_1)
    quarters = [share_0.astype(f32), share_1.astype(f32)]
    grad_qkv_shard = jnp.concatenate([part[index] for index in range(3) for part in quarters], axis=1)
    grad_out_shard = jnp.concatenate([part[3] for part in quarters], axis=1)

    fc_bias_part = jnp.where(
        jnp.arange(4)[None, :, None] == rep, (sum_near + sum_far).reshape(shards, 1, shard_rows), 0.0
    )
    sums = [
        sums_one[0],
        sums_one[1],
        sums_one[2:],
        sums_two[2],
        sums_two[0],
        sums_two[1],
        fc_bias_part,
        sums_two[3],
    ]
    table = jnp.concatenate([item.reshape(shards, -1) for item in sums], axis=1)
    table = after(table, total_1)
    table = table + over_core(table)
    table = (table + over_x(table)).reshape(2, chips, -1)
    table = lax.dynamic_index_in_dim(table, dp, 0, keepdims=False) + over_y(
        lax.dynamic_index_in_dim(table, 1 - dp, 0, keepdims=False)
    )
    mine = jnp.sum(lax.all_to_all(table[:, None], "ctx", 0, 0, tiled=True), axis=(0, 1))
    small_out, at = [], 0
    for item in sums:
        count = item.size // shards
        small_out.append(mine[at : at + count])
        at += count
    return (
        block_out,
        input_grad,
        small_out[0],
        small_out[1],
        grad_qkv_shard,
        small_out[2],
        grad_out_shard,
        small_out[3],
        small_out[4],
        small_out[5],
        grad_fc_shard,
        small_out[6],
        grad_proj_shard,
        small_out[7],
    )


def local(hidden_in, *rest):
    seqs, block, _ = hidden_in.shape
    sizes = tuple(lax.axis_size(name) for name in ("rep", "dp", "ctx"))
    if sizes[:2] == (4, 2) and 2 * seqs == sizes[2] and sizes[2] * block == SEQ and block == PIECE:
        return sequence_local(hidden_in, *rest)
    return general_local(hidden_in, *rest)


def solution(mesh):
    placed = (
        P(("rep", "dp"), "ctx", None),
        P(("rep", "dp"), None),
        P(("rep", "dp"), "ctx", None),
        P(("dp", "ctx")),
        P(("dp", "ctx")),
        P(("dp", "ctx"), None),
        P(("dp", "ctx")),
        P(("dp", "ctx"), None),
        P(("dp", "ctx")),
        P(("dp", "ctx")),
        P(("dp", "ctx")),
        P(("dp", "ctx"), None),
        P(("dp", "ctx")),
        P(("dp", "ctx"), None),
        P(("dp", "ctx")),
    )
    return jax.shard_map(
        local,
        mesh=mesh,
        in_specs=placed,
        out_specs=(
            P(("rep", "dp"), "ctx", None),
            P(("rep", "dp"), "ctx", None),
            P(("dp", "ctx")),
            P(("dp", "ctx")),
            P(("dp", "ctx"), None),
            P(("dp", "ctx")),
            P(("dp", "ctx"), None),
            P(("dp", "ctx")),
            P(("dp", "ctx")),
            P(("dp", "ctx")),
            P(("dp", "ctx"), None),
            P(("dp", "ctx")),
            P(("dp", "ctx"), None),
            P(("dp", "ctx")),
        ),
        check_vma=False,
    )
```

```python
import jax
import jax.numpy as jnp
from jax import lax
from jax.experimental import pallas as pl
from jax.experimental.pallas import tpu as pltpu
from jax.sharding import PartitionSpec as P

D = 1600
HEADS = 25
HD = 64
FF = 6400
SEQ = 1024
PIECE = 256


EPSILON = 1e-05
MASKED = -1000000000.0
gelu_coeff = 0.7978845608028654
gelu_cubic = 0.044715


def layer_norm(values, gain, shift):
    center = values - jnp.mean(values, axis=-1, keepdims=True)
    inv_std = lax.rsqrt(jnp.mean(center * center, axis=-1, keepdims=True) + EPSILON)
    normed = center * inv_std
    return (normed * gain + shift, normed, inv_std)


def norm_back(upstream, normed, inv_std, gain):
    scaled = upstream * gain
    inner = (
        scaled
        - jnp.mean(scaled, axis=-1, keepdims=True)
        - normed * jnp.mean(scaled * normed, axis=-1, keepdims=True)
    )
    return (inner * inv_std, jnp.sum(upstream * normed, axis=0), jnp.sum(upstream, axis=0))


def gelu_both(values):
    tanh_value = jnp.tanh(gelu_coeff * (values + gelu_cubic * values * values * values))
    result = 0.5 * values * (1.0 + tanh_value)
    slope = 0.5 * (1.0 + tanh_value) + 0.5 * values * (
        1.0 - tanh_value * tanh_value
    ) * gelu_coeff * (1.0 + 3.0 * gelu_cubic * values * values)
    return (result, slope)


def visible(starts, row_pos, key_pos):
    row_in = (
        (row_pos[:, None] >= starts[None, :]) & (row_pos[:, None] < starts[None, :] + PIECE)
    ).astype(jnp.float32)
    key_in = (
        (key_pos[:, None] >= starts[None, :]) & (key_pos[:, None] < starts[None, :] + PIECE)
    ).astype(jnp.float32)
    shared = jnp.dot(row_in, key_in.T, preferred_element_type=jnp.float32) > 0.5
    return (key_pos[None, :] <= row_pos[:, None]) | shared


def head_scores(query_heads, keys_heads, allowed):
    scores = jnp.einsum(
        "thd,shd->hts", query_heads, keys_heads, preferred_element_type=jnp.float32
    ) * HD ** (-0.5)
    return jnp.where(allowed[None], scores, MASKED)


def general_local(
    hidden_in,
    piece_starts,
    grad_out,
    attn_gain,
    attn_shift,
    qkv_weight,
    qv_bias,
    out_weight,
    out_bias,
    mlp_gain,
    mlp_shift,
    fc_weight,
    fc_bias,
    proj_weight,
    proj_bias,
):
    row_count = hidden_in.shape[1]
    shard_rows = attn_gain.shape[0]
    row_pos = lax.axis_index("ctx") * row_count + jnp.arange(row_count, dtype=jnp.int32)
    key_pos = jnp.arange(SEQ, dtype=jnp.int32)
    scale = HD ** (-0.5)
    attn_shards = (attn_gain, attn_shift, qkv_weight, qv_bias, out_weight, out_bias)
    mlp_shards = (mlp_gain, mlp_shift, fc_weight, fc_bias, proj_weight, proj_bias)
    outputs = []
    input_grads = []
    kept_rows = []
    norm_totals = [jnp.zeros((D,), jnp.float32) for index in range(4)]
    for micro_index in range(hidden_in.shape[0]):
        attn_full = (
            lax.all_gather(attn_shards[0], ("dp", "ctx"), axis=0, tiled=True),
            lax.all_gather(attn_shards[1], ("dp", "ctx"), axis=0, tiled=True),
            lax.all_gather(attn_shards[2], ("dp", "ctx"), axis=0, tiled=True),
            lax.all_gather(attn_shards[3], ("dp", "ctx"), axis=0, tiled=True),
            lax.all_gather(attn_shards[4], ("dp", "ctx"), axis=0, tiled=True),
            lax.all_gather(attn_shards[5], ("dp", "ctx"), axis=0, tiled=True),
        )
        mlp_full = (
            lax.all_gather(mlp_shards[0], ("dp", "ctx"), axis=0, tiled=True),
            lax.all_gather(mlp_shards[1], ("dp", "ctx"), axis=0, tiled=True),
            lax.all_gather(mlp_shards[2], ("dp", "ctx"), axis=0, tiled=True),
            lax.all_gather(mlp_shards[3], ("dp", "ctx"), axis=0, tiled=True),
            lax.all_gather(mlp_shards[4], ("dp", "ctx"), axis=0, tiled=True),
            lax.all_gather(mlp_shards[5], ("dp", "ctx"), axis=0, tiled=True),
        )
        gain_one, shift_one, qkv_full, qv_full, out_full, out_bias_full = attn_full
        gain_two, shift_two, fc_full, fc_bias_full, proj_full, proj_bias_full = mlp_full
        tokens = hidden_in[micro_index].astype(jnp.float32)
        starts = piece_starts[micro_index]
        allowed = visible(starts, row_pos, key_pos)
        normed_out, normed_one, inv_one = layer_norm(
            tokens, gain_one.astype(jnp.float32), shift_one.astype(jnp.float32)
        )
        h1_low = normed_out.astype(jnp.bfloat16)
        qv_float = qv_full.astype(jnp.float32)
        full_bias = jnp.concatenate([qv_float[:D], jnp.zeros((D,), jnp.float32), qv_float[D:]])
        qkv_low = (
            jnp.dot(h1_low, qkv_full, preferred_element_type=jnp.float32) + full_bias
        ).astype(jnp.bfloat16)
        query_low = qkv_low[:, :D]
        keys_all, values_all = (
            lax.all_gather(qkv_low[:, D : 2 * D], "ctx", axis=0, tiled=True),
            lax.all_gather(qkv_low[:, 2 * D :], "ctx", axis=0, tiled=True),
        )
        query_heads = query_low.reshape(row_count, HEADS, HD)
        keys_heads = keys_all.reshape(SEQ, HEADS, HD)
        values_heads = values_all.reshape(SEQ, HEADS, HD)
        scores = head_scores(query_heads, keys_heads, allowed)
        top_score = jnp.max(scores, axis=-1, keepdims=True)
        expo = jnp.exp(scores - top_score)
        expo_sum = jnp.sum(expo, axis=-1, keepdims=True)
        probs_low = (expo / expo_sum).astype(jnp.bfloat16)
        log_total = top_score + jnp.log(expo_sum)
        mixed = jnp.einsum(
            "hts,shd->thd", probs_low, values_heads, preferred_element_type=jnp.float32
        )
        attn_low = mixed.reshape(row_count, D).astype(jnp.bfloat16)
        after_attn = (
            tokens
            + jnp.dot(attn_low, out_full, preferred_element_type=jnp.float32)
            + out_bias_full.astype(jnp.float32)
        )
        normed_out_two, normed_two, inv_two = layer_norm(
            after_attn, gain_two.astype(jnp.float32), shift_two.astype(jnp.float32)
        )
        h2_low = normed_out_two.astype(jnp.bfloat16)
        hidden_pre = jnp.dot(
            h2_low, fc_full, preferred_element_type=jnp.float32
        ) + fc_bias_full.astype(jnp.float32)
        hidden_act, hidden_slope = gelu_both(hidden_pre)
        act_low = hidden_act.astype(jnp.bfloat16)
        block_value = (
            after_attn
            + jnp.dot(act_low, proj_full, preferred_element_type=jnp.float32)
            + proj_bias_full.astype(jnp.float32)
        )
        outputs.append(block_value.astype(jnp.bfloat16))
        gain_two_back, fc_back, proj_back = (
            lax.all_gather(mlp_gain, ("dp", "ctx"), axis=0, tiled=True),
            lax.all_gather(fc_weight, ("dp", "ctx"), axis=0, tiled=True),
            lax.all_gather(proj_weight, ("dp", "ctx"), axis=0, tiled=True),
        )
        gain_one_back, qkv_back, out_back = (
            lax.all_gather(attn_gain, ("dp", "ctx"), axis=0, tiled=True),
            lax.all_gather(qkv_weight, ("dp", "ctx"), axis=0, tiled=True),
            lax.all_gather(out_weight, ("dp", "ctx"), axis=0, tiled=True),
        )
        cot_low = grad_out[micro_index]
        grad_act = jnp.einsum("td,fd->tf", cot_low, proj_back, preferred_element_type=jnp.float32)
        grad_pre_low = (grad_act * hidden_slope).astype(jnp.bfloat16)
        grad_h2 = jnp.einsum("tf,df->td", grad_pre_low, fc_back, preferred_element_type=jnp.float32)
        grad_through, grad_gain_two, grad_shift_two = norm_back(
            grad_h2, normed_two, inv_two, gain_two_back.astype(jnp.float32)
        )
        grad_after = grad_through + cot_low.astype(jnp.float32)
        grad_after_low = grad_after.astype(jnp.bfloat16)
        grad_attn_low = jnp.einsum(
            "te,de->td", grad_after_low, out_back, preferred_element_type=jnp.float32
        ).astype(jnp.bfloat16)
        grad_attn_heads = grad_attn_low.reshape(row_count, HEADS, HD)
        again_scores = head_scores(query_heads, keys_heads, allowed)
        probs = jnp.exp(again_scores - log_total)
        probs_again = probs.astype(jnp.bfloat16)
        grad_probs = jnp.einsum(
            "thd,shd->hts", grad_attn_heads, values_heads, preferred_element_type=jnp.float32
        )
        grad_scores_low = (
            probs * (grad_probs - jnp.sum(probs * grad_probs, axis=-1, keepdims=True))
        ).astype(jnp.bfloat16)
        grad_query = (
            jnp.einsum(
                "hts,shd->thd", grad_scores_low, keys_heads, preferred_element_type=jnp.float32
            )
            * scale
        )

        def key_value_term(
            start,
            count,
            grad_scores_low=grad_scores_low,
            probs_again=probs_again,
            query_heads=query_heads,
            grad_attn_heads=grad_attn_heads,
        ):
            grad_k = (
                jnp.einsum(
                    "hts,thd->shd", grad_scores_low, query_heads, preferred_element_type=jnp.float32
                )
                * scale
            )
            grad_v = jnp.einsum(
                "hts,thd->shd", probs_again, grad_attn_heads, preferred_element_type=jnp.float32
            )
            return jnp.concatenate([grad_k.reshape(count, D), grad_v.reshape(count, D)], axis=1)

        kv_summed = lax.psum_scatter(
            key_value_term(jnp.int32(0), lax.axis_size("ctx") * row_count).astype(jnp.bfloat16),
            "ctx",
            scatter_dimension=0,
            tiled=True,
        ).astype(jnp.float32)
        grad_qkv_low = jnp.concatenate(
            [grad_query.reshape(row_count, D), kv_summed], axis=1
        ).astype(jnp.bfloat16)
        grad_h1 = jnp.einsum(
            "te,de->td", grad_qkv_low, qkv_back, preferred_element_type=jnp.float32
        )
        grad_into, grad_gain_one, grad_shift_one = norm_back(
            grad_h1, normed_one, inv_one, gain_one_back.astype(jnp.float32)
        )
        input_grads.append(grad_after + grad_into)
        kept_rows.append(
            (h1_low, grad_qkv_low, attn_low, grad_after_low, h2_low, grad_pre_low, act_low, cot_low)
        )
        norm_totals = [
            norm_totals[0] + grad_gain_one,
            norm_totals[1] + grad_shift_one,
            norm_totals[2] + grad_gain_two,
            norm_totals[3] + grad_shift_two,
        ]
    (
        h1_rows,
        grad_qkv_rows,
        attn_rows,
        grad_after_rows,
        h2_rows,
        grad_pre_rows,
        act_rows,
        cot_rows,
    ) = [jnp.concatenate([item[index] for item in kept_rows], axis=0) for index in range(8)]
    grad_qkv_w = jnp.einsum("td,te->de", h1_rows, grad_qkv_rows, preferred_element_type=jnp.float32)
    grad_out_w = jnp.einsum(
        "td,te->de", attn_rows, grad_after_rows, preferred_element_type=jnp.float32
    )
    attn_matrices = lax.psum_scatter(
        jnp.concatenate([grad_qkv_w, grad_out_w], axis=1),
        ("dp", "ctx"),
        scatter_dimension=0,
        tiled=True,
    )
    grad_fc_w = jnp.einsum("td,tf->df", h2_rows, grad_pre_rows, preferred_element_type=jnp.float32)
    grad_proj_w = jnp.einsum("tf,td->fd", act_rows, cot_rows, preferred_element_type=jnp.float32)
    mlp_matrices = lax.psum_scatter(
        jnp.concatenate(
            [grad_fc_w, grad_proj_w.reshape(lax.axis_size(("dp", "ctx")) * shard_rows, 4 * D)],
            axis=1,
        ),
        ("dp", "ctx"),
        scatter_dimension=0,
        tiled=True,
    )
    column_sums = jnp.sum(grad_qkv_rows, axis=0, dtype=jnp.float32)
    grad_qv_b = jnp.concatenate([column_sums[:D], column_sums[2 * D :]])
    grad_out_b = jnp.sum(grad_after_rows, axis=0, dtype=jnp.float32)
    grad_fc_b = jnp.sum(grad_pre_rows, axis=0, dtype=jnp.float32)
    grad_proj_b = jnp.sum(cot_rows, axis=0, dtype=jnp.float32)
    small_sums = (
        lax.psum_scatter(norm_totals[0], ("dp", "ctx"), scatter_dimension=0, tiled=True),
        lax.psum_scatter(norm_totals[1], ("dp", "ctx"), scatter_dimension=0, tiled=True),
        lax.psum_scatter(grad_qv_b, ("dp", "ctx"), scatter_dimension=0, tiled=True),
        lax.psum_scatter(grad_out_b, ("dp", "ctx"), scatter_dimension=0, tiled=True),
        lax.psum_scatter(norm_totals[2], ("dp", "ctx"), scatter_dimension=0, tiled=True),
        lax.psum_scatter(norm_totals[3], ("dp", "ctx"), scatter_dimension=0, tiled=True),
        lax.psum_scatter(grad_fc_b, ("dp", "ctx"), scatter_dimension=0, tiled=True),
        lax.psum_scatter(grad_proj_b, ("dp", "ctx"), scatter_dimension=0, tiled=True),
    )
    grad_qkv_shard = attn_matrices[:, : 3 * D]
    grad_out_shard = attn_matrices[:, 3 * D :]
    grad_fc_shard = mlp_matrices[:, :FF]
    grad_proj_shard = mlp_matrices[:, FF:].reshape(4 * shard_rows, D)
    summed = (
        lax.psum(small_sums[0].astype(jnp.bfloat16), "rep").astype(jnp.float32),
        lax.psum(small_sums[1].astype(jnp.bfloat16), "rep").astype(jnp.float32),
        lax.psum(grad_qkv_shard.astype(jnp.bfloat16), "rep").astype(jnp.float32),
        lax.psum(small_sums[2].astype(jnp.bfloat16), "rep").astype(jnp.float32),
        lax.psum(grad_out_shard.astype(jnp.bfloat16), "rep").astype(jnp.float32),
        lax.psum(small_sums[3].astype(jnp.bfloat16), "rep").astype(jnp.float32),
        lax.psum(small_sums[4].astype(jnp.bfloat16), "rep").astype(jnp.float32),
        lax.psum(small_sums[5].astype(jnp.bfloat16), "rep").astype(jnp.float32),
        lax.psum(grad_fc_shard.astype(jnp.bfloat16), "rep").astype(jnp.float32),
        lax.psum(small_sums[6].astype(jnp.bfloat16), "rep").astype(jnp.float32),
        lax.psum(grad_proj_shard.astype(jnp.bfloat16), "rep").astype(jnp.float32),
        lax.psum(small_sums[7].astype(jnp.bfloat16), "rep").astype(jnp.float32),
    )
    return (
        jnp.stack(outputs),
        jnp.stack(input_grads),
        summed[0],
        summed[1],
        summed[2],
        summed[3],
        summed[4],
        summed[5],
        summed[6],
        summed[7],
        summed[8],
        summed[9],
        summed[10],
        summed[11],
    )


LANES = 128
SUBLANES = 8
GRANT = 58 << 20
NO_COST = pl.CostEstimate(flops=1, transcendentals=0, bytes_accessed=1)


def permuted(value, axis, pairs):
    if value.ndim < 2 or value.shape[-2] % SUBLANES:
        return lax.ppermute(value, axis, pairs)
    rows = value.reshape(-1, SUBLANES, value.shape[-1])
    return lax.ppermute(rows, axis, pairs).reshape(value.shape)


def over_core(value):
    return permuted(value, "rep", [(0, 1), (1, 0), (2, 3), (3, 2)])


def over_x(value):
    return permuted(value, "rep", [(0, 2), (2, 0), (1, 3), (3, 1)])


def over_y(value):
    return permuted(value, "dp", [(0, 1), (1, 0)])


def ordered(first_is_mine, mine, other):
    return jnp.stack(
        [jnp.where(first_is_mine, mine, other), jnp.where(first_is_mine, other, mine)]
    )


def mxu(left, right, dims=((1,), (0,))):
    return lax.dot_general(left, right, (dims, ((), ())), preferred_element_type=jnp.float32)


def after(value, *others):
    return lax.optimization_barrier((value, *others))[0]


def half_rows(index, core, half):
    mine = (core + index) % 2
    start = 2 * half * index
    return (
        pl.ds(pl.multiple_of(start + half * mine, half), half),
        pl.ds(pl.multiple_of(start + half * (1 - mine), half), half),
    )


def in_sequence(core, valid, mine_ref, other_ref, whole):
    half = mine_ref.shape[0] // CHUNKS
    for index in range(CHUNKS):
        mine, other = half_rows(index, core, half)
        rows = slice(index * half, (index + 1) * half)
        whole[mine, :] = jnp.where(valid, mine_ref[rows, :], 0)
        whole[other, :] = jnp.where(valid, other_ref[rows, :], 0)


def masked_scores(keys, queries, first, count, limit):
    scores = mxu(keys[:count], queries, ((1,), (1,)))
    position = first + lax.broadcasted_iota(jnp.int32, (count - first, queries.shape[0]), 0)
    tail = jnp.where(position < limit, scores[first:], MASKED)
    return tail if first == 0 else jnp.concatenate([scores[:first], tail], axis=0)


def attend_forward_kernel(
    core_ref, limit_ref, q_ref, k_ref, k_other_ref, v_ref, v_other_ref, o_ref, lse_ref, k_all, v_all
):
    pair = pl.program_id(0)
    width = q_ref.shape[0] // 2
    lane = lax.broadcasted_iota(jnp.int32, (1, LANES), 1)
    valid = lane < D - pair * LANES
    queries = jnp.where(valid, q_ref[...], 0) * jnp.asarray(HD ** (-0.5), q_ref.dtype)
    in_sequence(core_ref[0], valid, k_ref, k_other_ref, k_all)
    in_sequence(core_ref[0], valid, v_ref, v_other_ref, v_all)
    keys = k_all[...]
    values_t = v_all[...].T
    for part in range(2):
        rows = slice(part * width, (part + 1) * width)
        first, count = KEY_SPANS[part]
        mixed = []
        for head in range(2):
            own = (lane >= head * HD) & (lane < (head + 1) * HD)
            scores = masked_scores(
                keys, jnp.where(own, queries[rows], 0), first, count, limit_ref[:, rows]
            )
            top = jnp.max(scores, axis=0, keepdims=True)
            expo = jnp.exp(scores - top)
            total = jnp.sum(expo, axis=0, keepdims=True)
            values = values_t[head * HD : (head + 1) * HD, :count]
            mixed.append(mxu(values, expo.astype(jnp.bfloat16)) / total)
            lse_ref[0, head : head + 1, rows] = top + jnp.log(total)
        o_ref[rows, :] = jnp.concatenate(mixed, axis=0).T.astype(o_ref.dtype)


def attend_backward_kernel(
    start,
    core_ref,
    limit_ref,
    q_ref,
    k_ref,
    k_other_ref,
    v_ref,
    v_other_ref,
    grad_ref,
    after_ref,
    lse_ref,
    dq_ref,
    dk_ref,
    dk_other_ref,
    dv_ref,
    dv_other_ref,
    send_a_ref,
    send_b_ref,
    k_all,
    v_all,
    dk_sum,
    dv_sum,
):
    pair = pl.program_id(0) + start
    width = q_ref.shape[0] // 2
    lane = lax.broadcasted_iota(jnp.int32, (1, LANES), 1)
    valid = lane < D - pair * LANES
    queries = jnp.where(valid, q_ref[...], 0) * jnp.asarray(HD ** (-0.5), q_ref.dtype)
    grads = jnp.where(valid, grad_ref[...], 0)
    core = core_ref[0]
    in_sequence(core, valid, k_ref, k_other_ref, k_all)
    in_sequence(core, valid, v_ref, v_other_ref, v_all)
    keys = k_all[...]
    keys_t = keys.T
    values = v_all[...]
    for part in (1, 0):
        rows = slice(part * width, (part + 1) * width)
        first, count = KEY_SPANS[part]
        grad_q, grad_k, grad_v = [], 0.0, 0.0
        for head in range(2):
            own = (lane >= head * HD) & (lane < (head + 1) * HD)
            queries_own = jnp.where(own, queries[rows], 0)
            grads_own = jnp.where(own, grads[rows], 0)
            scores = masked_scores(keys, queries_own, first, count, limit_ref[:, rows])
            probs = jnp.exp(scores - lse_ref[0, head : head + 1, rows])
            grad_probs = mxu(values[:count], grads_own, ((1,), (1,)))
            inner = jnp.sum(probs * grad_probs, axis=0, keepdims=True)
            grad_scores = (probs * (grad_probs - inner)).astype(jnp.bfloat16)
            grad_q.append(mxu(keys_t[head * HD : (head + 1) * HD, :count], grad_scores))
            grad_k += mxu(grad_scores, queries_own)
            grad_v += mxu(probs.astype(jnp.bfloat16), grads_own)
        grad_q = jnp.concatenate(grad_q, axis=0) * HD ** (-0.5)
        dq_ref[rows, :] = grad_q.T.astype(dq_ref.dtype)
        if part == 1:
            dk_sum[...] = grad_k
            dv_sum[...] = grad_v
        else:
            dk_sum[:count, :] += grad_k
            dv_sum[:count, :] += grad_v
    half = dk_ref.shape[0] // CHUNKS
    for index in range(CHUNKS):
        mine, other = half_rows(index, core, half)
        at = slice(index * half, (index + 1) * half)
        dk_ref[at, :] = dk_sum[mine, :].astype(dk_ref.dtype)
        dk_other_ref[at, :] = dk_sum[other, :].astype(dk_ref.dtype)
        dv_ref[at, :] = dv_sum[mine, :].astype(dv_ref.dtype)
        dv_other_ref[at, :] = dv_sum[other, :].astype(dv_ref.dtype)

    @pl.when(core == 0)
    def _():
        send_a_ref[...] = dv_ref[...]
        send_b_ref[...] = after_ref[...]

    @pl.when(core == 1)
    def _():
        send_a_ref[...] = dq_ref[...]
        send_b_ref[...] = dk_ref[...]


CHUNKS = SEQ // PIECE
PAIRS = -(-D // LANES)
GROUPS = ((0, 7), (7, PAIRS))
KEY_SPANS = ((0, 640), (512, 1024))


def by_columns(rows, start=0):
    return pl.BlockSpec((rows, LANES), lambda pair: (0, pair + start))


def attend_forward(core, limit, q, k, k_other, v, v_other):
    rows = q.shape[0]
    return pl.pallas_call(
        attend_forward_kernel,
        grid=(PAIRS,),
        in_specs=[
            pl.BlockSpec(memory_space=pltpu.SMEM),
            pl.BlockSpec((1, rows), lambda pair: (0, 0)),
        ]
        + [by_columns(rows)] * 5,
        out_specs=[by_columns(rows), pl.BlockSpec((1, 2, rows), lambda pair: (pair, 0, 0))],
        out_shape=[
            jax.ShapeDtypeStruct((rows, D), jnp.bfloat16),
            jax.ShapeDtypeStruct((PAIRS, 2, rows), jnp.float32),
        ],
        scratch_shapes=[pltpu.VMEM((2 * rows, LANES), jnp.bfloat16)] * 2,
        cost_estimate=NO_COST,
        compiler_params=pltpu.CompilerParams(vmem_limit_bytes=GRANT),
        name="attend_forward",
    )(core, limit, q, k, k_other, v, v_other)


def attend_backward(group, core, limit, q, k, k_other, v, v_other, grad, grad_after, lse):
    rows = q.shape[0]
    start, stop = group
    columns = min(D, stop * LANES) - start * LANES
    return pl.pallas_call(
        lambda *refs: attend_backward_kernel(start, *refs),
        grid=(stop - start,),
        in_specs=[
            pl.BlockSpec(memory_space=pltpu.SMEM),
            pl.BlockSpec((1, rows), lambda pair: (0, 0)),
        ]
        + [by_columns(rows, start)] * 7
        + [pl.BlockSpec((1, 2, rows), lambda pair: (pair + start, 0, 0))],
        out_specs=[by_columns(rows)] * 7,
        out_shape=[jax.ShapeDtypeStruct((rows, columns), jnp.bfloat16)] * 7,
        scratch_shapes=[pltpu.VMEM((2 * rows, LANES), jnp.bfloat16)] * 2
        + [pltpu.VMEM((2 * rows, LANES), jnp.float32)] * 2,
        cost_estimate=NO_COST,
        compiler_params=pltpu.CompilerParams(vmem_limit_bytes=GRANT),
        name="attend_backward",
    )(core, limit, q, k, k_other, v, v_other, grad, grad_after, lse)


def weight_gradient_kernel(count, place_ref, *refs):
    lefts, rights = list(refs[:count]), list(refs[count:-3])
    send_ref, keep_ref, whole = refs[-3:]
    block = lefts[0].shape[1]
    total, left_at, right_at = 0.0, 0, 0
    while lefts:
        rows = min(lefts[0].shape[0] - left_at, rights[0].shape[0] - right_at)
        left = lefts[0][left_at : left_at + rows, :]
        total += mxu(left, rights[0][right_at : right_at + rows, :], ((0,), (0,)))
        left_at, right_at = left_at + rows, right_at + rows
        if left_at == lefts[0].shape[0]:
            lefts, left_at = lefts[1:], 0
        if right_at == rights[0].shape[0]:
            rights, right_at = rights[1:], 0
    step = pl.program_id(0)
    whole[pl.ds(pl.multiple_of(step * block, block), block), :] = total.astype(whole.dtype)

    @pl.when(step == pl.num_programs(0) - 1)
    def _():
        rows, dp = send_ref.shape[0], place_ref[1]
        send_ref[...] = whole[pl.ds(pl.multiple_of((1 - dp) * rows, rows), rows), :]
        keep_ref[...] = whole[pl.ds(pl.multiple_of(dp * rows, rows), rows), :]


def weight_gradient(place, lefts, rights, block=256):
    inner, outer = lefts[0].shape[1], rights[0].shape[1]
    steps = pl.cdiv(inner, block)
    return pl.pallas_call(
        lambda *refs: weight_gradient_kernel(len(lefts), *refs),
        grid=(steps,),
        in_specs=[pl.BlockSpec(memory_space=pltpu.SMEM)]
        + [pl.BlockSpec((left.shape[0], block), lambda i: (0, i)) for left in lefts]
        + [
            pl.BlockSpec(right.shape, lambda i: (0, 0), pipeline_mode=pl.Buffered(1))
            for right in rights
        ],
        out_specs=[pl.BlockSpec((inner // 2, outer), lambda i: (0, 0))] * 2,
        out_shape=[jax.ShapeDtypeStruct((inner // 2, outer), jnp.bfloat16)] * 2,
        scratch_shapes=[pltpu.VMEM((steps * block, outer), jnp.bfloat16)],
        cost_estimate=NO_COST,
        compiler_params=pltpu.CompilerParams(vmem_limit_bytes=GRANT),
        name="weight_gradient",
    )(place, *lefts, *rights)


def pair_sum_kernel(first_ref, second_ref, out_ref):
    total = first_ref[...].astype(jnp.float32) + second_ref[...].astype(jnp.float32)
    out_ref[...] = total.astype(out_ref.dtype)


def pair_sum(first, second, block=200):
    spec = pl.BlockSpec((block, first.shape[1]), lambda i: (i, 0))
    return pl.pallas_call(
        pair_sum_kernel,
        grid=(first.shape[0] // block,),
        in_specs=[spec, spec],
        out_specs=spec,
        out_shape=jax.ShapeDtypeStruct(first.shape, first.dtype),
        cost_estimate=NO_COST,
        compiler_params=pltpu.CompilerParams(vmem_limit_bytes=GRANT),
        name="pair_sum",
    )(first, second)


def second_terms_kernel(place_ref, *refs):
    came_x, came_y, kept_x, kept_y, send_x, send_y, stay_x, stay_y = refs
    dp, chip_x = place_ref[1], place_ref[0] // 2
    f32 = jnp.float32
    for kept, came, own, send, stay in (
        (kept_x, came_x, dp, send_x, stay_x),
        (kept_y, came_y, chip_x, send_y, stay_y),
    ):
        send[...] = (kept[1 - own].astype(f32) + came[1 - own].astype(f32)).astype(send.dtype)
        stay[...] = (kept[own].astype(f32) + came[own].astype(f32)).astype(send.dtype)


def second_terms(place, came_x, came_y, kept_x, kept_y):
    shape = jax.ShapeDtypeStruct(came_x.shape[1:], came_x.dtype)
    return pl.pallas_call(
        second_terms_kernel,
        in_specs=[pl.BlockSpec(memory_space=pltpu.SMEM)]
        + [pl.BlockSpec(memory_space=pltpu.VMEM)] * 4,
        out_specs=[pl.BlockSpec(memory_space=pltpu.VMEM)] * 4,
        out_shape=[shape] * 4,
        cost_estimate=NO_COST,
        compiler_params=pltpu.CompilerParams(vmem_limit_bytes=GRANT),
        name="second_terms",
    )(place, came_x, came_y, kept_x, kept_y)


def summed_kernel(came_x, came_y, stay_x, stay_y, out_ref):
    rows = stay_x.shape[0]
    f32 = jnp.float32
    out_ref[:rows, :] = (stay_x[...].astype(f32) + came_x[...].astype(f32)).astype(out_ref.dtype)
    out_ref[rows:, :] = (stay_y[...].astype(f32) + came_y[...].astype(f32)).astype(out_ref.dtype)


def summed(came_x, came_y, stay_x, stay_y):
    rows, width = stay_x.shape
    return pl.pallas_call(
        summed_kernel,
        in_specs=[pl.BlockSpec(memory_space=pltpu.VMEM)] * 4,
        out_specs=pl.BlockSpec(memory_space=pltpu.VMEM),
        out_shape=jax.ShapeDtypeStruct((2 * rows, width), stay_x.dtype),
        cost_estimate=NO_COST,
        compiler_params=pltpu.CompilerParams(vmem_limit_bytes=GRANT),
        name="summed",
    )(came_x, came_y, stay_x, stay_y)


def block_value_kernel(after_ref, own_ref, core_ref, far_ref, bias_ref, out_ref):
    f32 = jnp.float32
    value = after_ref[...] + own_ref[...].astype(f32) + core_ref[...].astype(f32)
    out_ref[...] = (value + far_ref[...].astype(f32) + bias_ref[...]).astype(out_ref.dtype)


def block_value_of(after_attn, own, core, far, bias, block=128):
    spec = pl.BlockSpec((block, D), lambda i: (i, 0))
    return pl.pallas_call(
        block_value_kernel,
        grid=(own.shape[0] // block,),
        in_specs=[spec] * 4 + [pl.BlockSpec((1, D), lambda i: (0, 0))],
        out_specs=spec,
        out_shape=jax.ShapeDtypeStruct(own.shape, jnp.bfloat16),
        cost_estimate=NO_COST,
        compiler_params=pltpu.CompilerParams(vmem_limit_bytes=GRANT),
        name="block_value",
    )(after_attn, own, core, far, bias)


def attention_weights_kernel(
    place_ref,
    hidden_ref,
    hidden_other_ref,
    left_ref,
    left_other_ref,
    dq_ref,
    dk_ref,
    dk_other_ref,
    dv_ref,
    dv_other_ref,
    after_ref,
    key_came_ref,
    value_came_ref,
    came_a_ref,
    came_b_ref,
    send_x_ref,
    keep_x_ref,
    send_y_ref,
    keep_y_ref,
    right,
    terms,
):
    rep, dp = place_ref[0], place_ref[1]
    chip_x, core = rep // 2, rep % 2
    rows, width = dq_ref.shape
    low, f32 = jnp.bfloat16, jnp.float32
    own, other = slice(0, rows), slice(rows, 2 * rows)
    add = lambda first, second: (first[...].astype(f32) + second[...].astype(f32)).astype(low)

    @pl.when(core == 0)
    def _():
        right[0, own, :] = dq_ref[...]
        right[0, other, :] = came_a_ref[...]
        right[1, own, :] = add(dk_ref, key_came_ref)
        right[1, other, :] = add(dk_other_ref, came_b_ref)

    @pl.when(core == 1)
    def _():
        right[0, own, :] = add(dv_ref, value_came_ref)
        right[0, other, :] = add(dv_other_ref, came_a_ref)
        right[1, own, :] = after_ref[:, :width]
        right[1, other, :] = came_b_ref[...]

    for index, lefts in enumerate(((hidden_ref, hidden_other_ref), (left_ref, left_other_ref))):
        for at in range(0, D, 256):
            columns = slice(at, min(D, at + 256))
            term = mxu(lefts[0][:, columns], right[index, own, :], ((0,), (0,)))
            term += mxu(lefts[1][:, columns], right[index, other, :], ((0,), (0,)))
            terms[index, columns, :] = term.astype(low)
    quarter = D // 4
    for side in range(2):
        part = pl.ds(2 * side * quarter, quarter)
        send_x_ref[side] = terms[1 - chip_x, part, :]
        keep_x_ref[side] = terms[chip_x, part, :]
    for index in range(2):
        start = lambda at: pl.ds(pl.multiple_of((2 * at + 1) * quarter, quarter), quarter)
        send_y_ref[index] = terms[index, start(1 - dp), :]
        keep_y_ref[index] = terms[index, start(dp), :]


def attention_weights(place, hidden, hidden_other, left, left_other, grads, came):
    rows, width = grads[0].shape
    shape = jax.ShapeDtypeStruct((2, D // 4, width), jnp.bfloat16)
    arrays = [hidden, hidden_other, left, left_other, *grads, *came]
    return pl.pallas_call(
        attention_weights_kernel,
        in_specs=[pl.BlockSpec(memory_space=pltpu.SMEM)]
        + [pl.BlockSpec(memory_space=pltpu.VMEM)] * len(arrays),
        out_specs=[pl.BlockSpec(memory_space=pltpu.VMEM)] * 4,
        out_shape=[shape] * 4,
        scratch_shapes=[
            pltpu.VMEM((2, 2 * rows, width), jnp.bfloat16),
            pltpu.VMEM((2, D, width), jnp.bfloat16),
        ],
        cost_estimate=NO_COST,
        compiler_params=pltpu.CompilerParams(vmem_limit_bytes=GRANT),
        name="attention_weights",
    )(place, *arrays)


QUERY, VALUE, KEY, OUT = range(4)


def matrix_copies(place_ref, role, pieces, whole, sems):
    rep, dp = place_ref[0], place_ref[1]
    count = pieces[0].shape[0]
    copies = []
    for t in range(4):
        copies.append([])
        for side in range(2):
            start = pl.multiple_of((dp if side == 0 else 1 - dp) * count, count)
            copies[t].append(
                pltpu.make_async_copy(
                    pieces[2 * t + side], whole.at[pl.ds(start, count), :], sems.at[side]
                )
            )

    def start():
        for t in range(4):

            @pl.when((rep ^ t) == role)
            def _():
                copies[t][0].start()
                copies[t][1].start()

    def wait():
        copies[0][0].wait()
        copies[0][1].wait()

    return start, wait


def row_norm(values):
    center = values - jnp.mean(values, axis=-1, keepdims=True)
    inv_std = lax.rsqrt(jnp.mean(center * center, axis=-1, keepdims=True) + EPSILON)
    return center * inv_std, inv_std


def row_norm_back(upstream, normed, inv_std, gain):
    scaled = upstream * gain
    inner = (
        scaled
        - jnp.mean(scaled, axis=-1, keepdims=True)
        - normed * jnp.mean(scaled * normed, axis=-1, keepdims=True)
    )
    return inner * inv_std


def column_sum(values):
    return jnp.sum(values, axis=0, keepdims=True)


STRIP = 128


def strips(ref):
    return [slice(at, at + STRIP) for at in range(0, ref.shape[0], STRIP)]


def project_kernel(place_ref, tokens_ref, gain_ref, shift_ref, bias_ref, *refs):
    pieces, (h_ref, q_ref, k_ref, v_ref, weights, sems) = refs[:8], refs[8:]
    loads = [
        matrix_copies(place_ref, role, pieces, weights.at[slot], sems.at[slot])
        for slot, role in enumerate((QUERY, VALUE, KEY))
    ]
    for start, _ in loads:
        start()
    for rows in strips(tokens_ref):
        normed, _ = row_norm(tokens_ref[rows, :].astype(jnp.float32))
        h_ref[rows, :] = (normed * gain_ref[...] + shift_ref[...]).astype(h_ref.dtype)
    hidden = h_ref[...]
    loads[0][1]()
    q_ref[...] = (mxu(hidden, weights[0]) + bias_ref[:, :D]).astype(q_ref.dtype)
    loads[1][1]()
    v_ref[...] = (mxu(hidden, weights[1]) + bias_ref[:, D:]).astype(v_ref.dtype)
    loads[2][1]()
    k_ref[...] = mxu(hidden, weights[2]).astype(k_ref.dtype)


def out_kernel(place_ref, attn_ref, hidden_ref, tokens_ref, bias_ref, gain_ref, shift_ref, *refs):
    pieces, (x_ref, h_ref, left_ref, send_ref, weight, sems) = refs[:8], refs[8:]
    start, wait = matrix_copies(place_ref, OUT, pieces, weight, sems)
    start()
    low_core = place_ref[0] % 2 == 0
    left_ref[...] = jnp.where(low_core, hidden_ref[...], attn_ref[...])
    send_ref[...] = jnp.where(low_core, attn_ref[...], hidden_ref[...])
    wait()
    x_ref[...] = mxu(attn_ref[...], weight[...])
    for rows in strips(x_ref):
        value = tokens_ref[rows, :].astype(jnp.float32) + x_ref[rows, :] + bias_ref[...]
        x_ref[rows, :] = value
        normed, _ = row_norm(value)
        h_ref[rows, :] = (normed * gain_ref[...] + shift_ref[...]).astype(h_ref.dtype)


def out_back_kernel(place_ref, own_ref, core_ref, far_ref, x_ref, cot_ref, gain_ref, *refs):
    pieces, (after_ref, low_ref, grad_ref, sum_ref, weight, sems) = refs[:8], refs[8:]
    start, wait = matrix_copies(place_ref, OUT, pieces, weight, sems)
    start()
    f32 = jnp.float32
    totals = [0.0] * 4
    for rows in strips(x_ref):
        grad_h = own_ref[rows, :].astype(f32) + core_ref[rows, :].astype(f32)
        grad_h += far_ref[rows, :].astype(f32)
        normed, inv_std = row_norm(x_ref[rows, :])
        value = row_norm_back(grad_h, normed, inv_std, gain_ref[...]) + cot_ref[rows, :].astype(f32)
        after_ref[rows, :] = value
        value_low = value.astype(low_ref.dtype)
        low_ref[rows, :] = value_low
        terms = (grad_h * normed, grad_h, value_low.astype(f32), cot_ref[rows, :].astype(f32))
        totals = [total + column_sum(term) for total, term in zip(totals, terms)]
    for index, total in enumerate(totals):
        sum_ref[index : index + 1, :] = total
    wait()
    grad_ref[...] = mxu(low_ref[...], weight[...], ((1,), (1,))).astype(grad_ref.dtype)


def project_back_kernel(groups, place_ref, tokens_ref, after_ref, gain_ref, *refs):
    count = 5 * len(groups)
    grads, pieces = refs[:count], refs[count : count + 8]
    out_ref, sum_ref, weights, grad_h, sems = refs[count + 8 :]
    f32 = jnp.float32
    loads = [
        matrix_copies(place_ref, role, pieces, weights.at[slot], sems.at[slot])
        for slot, role in enumerate((QUERY, VALUE, KEY))
    ]
    for start, _ in loads:
        start()
    for slot in range(3):
        loads[slot][1]()
        for index, columns in enumerate(groups):
            query, value, value_came, key, key_came = grads[5 * index : 5 * index + 5]
            if slot == 0:
                grad = query[...]
            else:
                near, came = (value, value_came) if slot == 1 else (key, key_came)
                grad = (near[...].astype(f32) + came[...].astype(f32)).astype(query.dtype)
            term = mxu(grad, weights[slot, :, columns], ((1,), (1,)))
            if slot == 0 and index == 0:
                grad_h[...] = term
            else:
                grad_h[...] += term
            if slot < 2:
                sum_ref[2 + slot : 3 + slot, columns] = column_sum(grad.astype(f32))
    totals = [0.0, 0.0]
    for rows in strips(tokens_ref):
        upstream = grad_h[rows, :]
        normed, inv_std = row_norm(tokens_ref[rows, :].astype(f32))
        value = row_norm_back(upstream, normed, inv_std, gain_ref[...]) + after_ref[rows, :]
        out_ref[rows, :] = value.astype(out_ref.dtype)
        terms = (upstream * normed, upstream)
        totals = [total + column_sum(term) for total, term in zip(totals, terms)]
    for index, total in enumerate(totals):
        sum_ref[index : index + 1, :] = total


def on_chip(body, name, place, arrays, pieces, outs, scratch):
    return pl.pallas_call(
        body,
        in_specs=[pl.BlockSpec(memory_space=pltpu.SMEM)]
        + [pl.BlockSpec(memory_space=pltpu.VMEM)] * len(arrays)
        + [pl.BlockSpec(memory_space=pl.ANY)] * len(pieces),
        out_specs=[pl.BlockSpec(memory_space=pltpu.VMEM)] * len(outs),
        out_shape=[jax.ShapeDtypeStruct(*out) for out in outs],
        scratch_shapes=scratch,
        cost_estimate=NO_COST,
        compiler_params=pltpu.CompilerParams(vmem_limit_bytes=GRANT),
        name=name,
    )(place, *arrays, *pieces)


def feed_forward_kernel(place_ref, *refs):
    h_ref, h_core_ref, cot_ref, cot_core_ref, bias_ref, *refs = refs
    pieces, refs = refs[:4], refs[4:]
    act_ref, pre_ref, out_ref, out_core_ref, back_ref, back_core_ref, sum_ref, fc, proj, sems = refs
    step = pl.program_id(0)
    dp = place_ref[1]

    @pl.when(step == 0)
    def _():
        copies = []
        for index, piece in enumerate(pieces):
            whole = fc if index < 2 else proj
            count = piece.shape[0]
            start = pl.multiple_of((dp if index % 2 == 0 else 1 - dp) * count, count)
            copies.append(
                pltpu.make_async_copy(piece, whole.at[pl.ds(start, count), :], sems.at[index])
            )
        for copy in copies:
            copy.start()
        for copy in copies:
            copy.wait()
        sum_ref[...] = jnp.zeros_like(sum_ref)

    own = step < pl.num_programs(0) // 2
    hidden = jnp.where(own, h_ref[...], h_core_ref[...])
    cotangent = jnp.where(own, cot_ref[...], cot_core_ref[...])
    hidden_act, hidden_slope = gelu_both(mxu(hidden, fc[...]) + bias_ref[...])
    act_low = hidden_act.astype(jnp.bfloat16)
    act_ref[...] = act_low
    out = mxu(act_low, proj[...]).astype(out_ref.dtype)
    grad_act = mxu(cotangent, proj[...], ((1,), (1,)))
    pre_low = (grad_act * hidden_slope).astype(jnp.bfloat16)
    pre_ref[...] = pre_low
    back = mxu(pre_low, fc[...], ((1,), (1,))).astype(back_ref.dtype)
    sum_ref[...] += column_sum(pre_low.astype(jnp.float32))

    @pl.when(own)
    def _():
        out_ref[...] = out
        back_ref[...] = back

    @pl.when(jnp.logical_not(own))
    def _():
        out_core_ref[...] = out
        back_core_ref[...] = back


def feed_forward(place, hidden, hidden_core, cot, cot_core, bias, pieces, block_rows=256):
    rows, units = hidden.shape[0], D
    steps = rows // block_rows
    first = pl.BlockSpec((block_rows, D), lambda i: (jnp.minimum(i, steps - 1), 0))
    second = pl.BlockSpec((block_rows, D), lambda i: (jnp.maximum(i - steps, 0), 0))
    by_block = pl.BlockSpec((block_rows, D), lambda i: (i, 0))
    return pl.pallas_call(
        feed_forward_kernel,
        grid=(2 * steps,),
        in_specs=[pl.BlockSpec(memory_space=pltpu.SMEM), first, second, first, second]
        + [pl.BlockSpec((1, units), lambda i: (0, 0))]
        + [pl.BlockSpec(memory_space=pl.ANY)] * 4,
        out_specs=[by_block, by_block, first, second, first, second]
        + [pl.BlockSpec((1, units), lambda i: (0, 0))],
        out_shape=[jax.ShapeDtypeStruct((2 * rows, D), jnp.bfloat16)] * 2
        + [jax.ShapeDtypeStruct((rows, D), jnp.bfloat16)] * 4
        + [jax.ShapeDtypeStruct((1, units), jnp.float32)],
        scratch_shapes=[pltpu.VMEM((D, D), jnp.bfloat16)] * 2 + [pltpu.SemaphoreType.DMA((4,))],
        cost_estimate=NO_COST,
        compiler_params=pltpu.CompilerParams(vmem_limit_bytes=GRANT),
        name="feed_forward",
    )(place, hidden, hidden_core, cot, cot_core, bias, *pieces)


def unpack_kernel(widths, rep_ref, small_ref, *out_refs):
    chips, count, _ = small_ref.shape
    shards = chips * count
    at = 0
    for width, out_ref in zip(widths, out_refs):
        pieces = [
            small_ref[shard % chips, shard // chips : shard // chips + 1, at : at + width]
            for shard in range(shards)
        ]
        at += width
        if width * shards == out_ref.shape[1]:
            out_ref[...] = jnp.concatenate(pieces, axis=1).astype(jnp.float32)
            continue
        part = width // 4
        for rep in range(4):

            @pl.when(rep_ref[0] == rep)
            def _():
                own = [piece[:, rep * part : (rep + 1) * part] for piece in pieces]
                out_ref[...] = jnp.concatenate(own, axis=1).astype(jnp.float32)


def unpack(rep, small, widths, picked):
    shards = small.shape[0] * small.shape[1]
    return pl.pallas_call(
        lambda *refs: unpack_kernel(widths, *refs),
        in_specs=[
            pl.BlockSpec(memory_space=pltpu.SMEM),
            pl.BlockSpec(memory_space=pltpu.VMEM),
        ],
        out_specs=[pl.BlockSpec(memory_space=pltpu.VMEM)] * len(widths),
        out_shape=[
            jax.ShapeDtypeStruct((1, width * shards // (4 if index == picked else 1)), jnp.float32)
            for index, width in enumerate(widths)
        ],
        cost_estimate=NO_COST,
        compiler_params=pltpu.CompilerParams(vmem_limit_bytes=GRANT),
        name="unpack",
    )(rep.astype(jnp.int32)[None], small)


def pick_kernel(rep_ref, whole_ref, part_ref):
    count = part_ref.shape[0]
    for rep in range(4):

        @pl.when(rep_ref[0] == rep)
        def _():
            pieces = [
                whole_ref[:, at : at + count] for at in range(rep * count, whole_ref.shape[1], 4 * count)
            ]
            part_ref[...] = jnp.concatenate(pieces, axis=1)


def pick_units(rep, whole):
    return pl.pallas_call(
        pick_kernel,
        in_specs=[
            pl.BlockSpec(memory_space=pltpu.SMEM),
            pl.BlockSpec(memory_space=pltpu.VMEM),
        ],
        out_specs=pl.BlockSpec(memory_space=pltpu.VMEM),
        out_shape=jax.ShapeDtypeStruct((whole.shape[0], whole.shape[1] // 4), whole.dtype),
        compiler_params=pltpu.CompilerParams(vmem_limit_bytes=GRANT),
        name="pick_units",
    )(rep.astype(jnp.int32)[None], whole)


def merge_kernel(parts_ref, whole_ref):
    count = parts_ref.shape[1]
    for at in range(0, parts_ref.shape[2], count):
        pieces = [parts_ref[core * 2 + x, :, at : at + count] for x in range(2) for core in range(2)]
        whole_ref[:, 4 * at : 4 * (at + count)] = jnp.concatenate(pieces, axis=1).astype(whole_ref.dtype)


def merge_units(parts):
    return pl.pallas_call(
        merge_kernel,
        in_specs=[pl.BlockSpec(memory_space=pltpu.VMEM)],
        out_specs=pl.BlockSpec(memory_space=pltpu.VMEM),
        out_shape=jax.ShapeDtypeStruct((parts.shape[1], 4 * parts.shape[2]), jnp.float32),
        compiler_params=pltpu.CompilerParams(vmem_limit_bytes=GRANT),
        name="merge_units",
    )(parts)


def sequence_local(
    hidden_in,
    piece_starts,
    grad_out,
    attn_gain,
    attn_shift,
    qkv_weight,
    qv_bias,
    out_weight,
    out_bias,
    mlp_gain,
    mlp_shift,
    fc_weight,
    fc_bias,
    proj_weight,
    proj_bias,
):
    rep, dp, ctx = (lax.axis_index(name) for name in ("rep", "dp", "ctx"))
    chip_x, core = rep // 2, rep % 2
    chips, shards = lax.axis_size("ctx"), lax.axis_size(("dp", "ctx"))
    seqs, block, _ = hidden_in.shape
    half = block // 2
    rows = chips * half
    shard_rows = D // shards
    f32, low = jnp.float32, jnp.bfloat16
    core_low, x_low, y_low = core == 0, chip_x == 0, dp == 0
    half_of = lambda index: (core + index) % 2

    def exchange(tiles):
        return lax.all_to_all(tiles, "ctx", 0, 0, tiled=True)

    def tiled(value):
        return value.reshape(chips, half // SUBLANES, SUBLANES, D)

    def by_sequence(value):
        halves = value.reshape(seqs, 2, half // SUBLANES, SUBLANES, D)
        mine = half_of(ctx)
        kept = lax.dynamic_index_in_dim(halves, mine, 1, keepdims=False)
        came = over_core(lax.dynamic_index_in_dim(halves, 1 - mine, 1, keepdims=False))
        return tiled(ordered(core_low, kept, came))

    def from_sequence(every):
        every = every.reshape(2, seqs, half // SUBLANES, SUBLANES, D)
        kept = lax.dynamic_index_in_dim(every, core, 0, keepdims=False)
        came = over_core(lax.dynamic_index_in_dim(every, 1 - core, 0, keepdims=False))
        both = ordered(half_of(ctx) == 0, kept, came)
        return both.transpose(1, 0, 2, 3, 4).reshape(seqs, block, D)

    def along_ctx(shard):
        return lax.all_gather(shard, "ctx", axis=0, tiled=True)

    items = (attn_gain, attn_shift, qv_bias, out_bias, mlp_gain, mlp_shift, fc_bias, proj_bias)
    small = jnp.concatenate(items)[None]
    small = ordered(y_low, small, over_y(small)).reshape(1, 2, -1)
    small = lax.all_to_all(
        jnp.broadcast_to(small, (chips,) + small.shape[1:]), "ctx", 0, 0, tiled=True
    )

    shard_attn = jnp.where(
        x_low,
        jnp.where(core_low, qkv_weight[:, :D], qkv_weight[:, 2 * D :]),
        jnp.where(core_low, qkv_weight[:, D : 2 * D], out_weight),
    )
    shard_fc = pick_units(rep, fc_weight)
    shard_proj = lax.dynamic_index_in_dim(
        proj_weight.reshape(4, shard_rows, D), rep, 0, keepdims=False
    )
    mine = along_ctx(shard_attn)
    tokens_sent = by_sequence(after(hidden_in, shard_attn))
    cot_sent = by_sequence(after(grad_out, tokens_sent))
    tokens_low = exchange(tokens_sent).reshape(rows, D)
    mine_fc = along_ctx(shard_fc)
    mine_proj = along_ctx(shard_proj)

    every_starts = ordered(core_low, piece_starts, over_core(piece_starts)).reshape(chips, -1)
    starts = lax.dynamic_index_in_dim(every_starts, ctx, 0, keepdims=False)
    block_index = jnp.arange(chips)
    row_pos = (
        (block_index * block + half_of(block_index) * half)[:, None] + jnp.arange(half)[None, :]
    ).reshape(rows)
    inside = (row_pos[:, None] >= starts[None, :]) & (row_pos[:, None] < starts[None, :] + PIECE)
    limit = jnp.maximum(row_pos + 1, jnp.max(jnp.where(inside, starts[None, :] + PIECE, 0), axis=1))
    limit = limit.astype(jnp.int32)[None, :]
    core_id = core.astype(jnp.int32)[None]

    place = jnp.stack([rep, dp]).astype(jnp.int32)

    vectors = unpack(rep, small, [item.shape[0] for item in items], 6)
    mine, vectors = lax.optimization_barrier(
        (mine, vectors, shard_fc, shard_proj, tokens_low, cot_sent, limit)
    )[:2]
    gain_one, shift_one, qv_full, out_bias_full, gain_two, shift_two, fc_bias_mine, proj_bias_full = vectors
    other, mine_x = lax.optimization_barrier((over_y(mine), over_x(mine)))
    cot_low = exchange(after(cot_sent, mine_fc)).reshape(rows, D)
    other_x, cot_low, fc_other = lax.optimization_barrier((over_x(other), cot_low, over_y(mine_fc)))
    pieces = []
    for pair in ((mine, other), (mine_x, other_x)):
        pieces += [pair[0], pair[1], over_core(pair[0]), over_core(pair[1])]

    h1_low, query_low, key_low, value_low = on_chip(
        project_kernel,
        "project",
        place,
        [tokens_low] + [gain_one, shift_one, qv_full],
        pieces,
        [((rows, D), low)] * 4,
        [pltpu.VMEM((3, D, D), low), pltpu.SemaphoreType.DMA((3, 2))],
    )
    key_other, value_other = over_core(key_low), over_core(value_low)
    proj_other = over_y(mine_proj)
    query_low = after(query_low, mine_proj)
    attn_low, lse = attend_forward(
        core_id, limit, query_low, key_low, key_other, value_low, value_other
    )
    cot_x, cot_core = over_x(cot_low), over_core(cot_low)
    after_attn, h2_low, left_b, send_b = on_chip(
        out_kernel,
        "attention_out",
        place,
        [after(attn_low, cot_x, proj_other), h1_low, tokens_low, out_bias_full, gain_two, shift_two],
        pieces,
        [((rows, D), f32)] + [((rows, D), low)] * 3,
        [pltpu.VMEM((D, D), low), pltpu.SemaphoreType.DMA((2,))],
    )

    h2_x, h2_core = over_x(h2_low), over_core(h2_low)
    proj_other = after(proj_other, h2_core)
    pieces_fc = [mine_fc, fc_other, mine_proj, proj_other]
    act_near, pre_near, out_near, out_core, back_near, back_core, sum_near = feed_forward(
        place, h2_low, h2_core, cot_low, cot_core, fc_bias_mine, pieces_fc
    )
    cot_x = after(cot_x, back_near)
    h2_x = after(h2_x, cot_x)
    cot_xc, h2_xc = over_core(cot_x), over_core(h2_x)
    act_far, pre_far, out_x, out_xc, back_x, back_xc, sum_far = feed_forward(
        place, h2_x, h2_xc, cot_x, cot_xc, fc_bias_mine, pieces_fc
    )

    def far_sum(own, core):
        return pair_sum(own, over_core(core), 128)

    back_x = far_sum(back_x, back_xc)
    back_came = over_x(back_x)
    back_core = over_core(back_core)
    out_x = far_sum(out_x, out_xc)
    act_near, pre_near = after((act_near, pre_near), back_x, out_x, back_core)
    proj_send, proj_kept = weight_gradient(
        place, [act_near, act_far], [cot_low, cot_core, cot_x, cot_xc])
    back_came = after(back_came, proj_send)
    out_came, out_core = over_x(after(out_x, back_came)), over_core(out_core)
    grad_after, grad_after_low, grad_attn_low, sums_two = on_chip(
        out_back_kernel,
        "attention_out_back",
        place,
        [back_near, back_core, back_came, after_attn, cot_low, gain_two],
        pieces,
        [((rows, D), f32), ((rows, D), low), ((rows, D), low), ((4, D), f32)],
        [pltpu.VMEM((D, D), low), pltpu.SemaphoreType.DMA((2,))],
    )

    proj_came = over_y(after(proj_send, back_came))

    def finish(value):
        return lax.psum_scatter(value, "ctx", scatter_dimension=0, tiled=True)

    def share(value):
        pair = ordered(x_low, value, over_x(value))
        return ordered(core_low, pair, over_core(pair)).reshape((4,) + value.shape)

    h1_other, left_b_other = over_core(h1_low), over_core(send_b)

    grads, terms = [], []
    held, spans = (), []
    for group in GROUPS:
        columns = slice(group[0] * LANES, min(D, group[1] * LANES))
        spans.append(columns)
        dq, dk, dk_other, dv, dv_other, send_one, send_two = attend_backward(
            group,
            core_id,
            limit,
            query_low,
            key_low,
            key_other,
            value_low,
            value_other,
            after(grad_attn_low, *held),
            grad_after_low,
            lse,
        )
        crossing = (dk_other, dv_other, send_one, send_two)
        came = [over_core(item) for item in crossing]
        if not group[0]:
            pre_near = after(pre_near, dq, out_came)
            fc_send, fc_kept = weight_gradient(
                place, [h2_low, h2_core, h2_x, h2_xc], [pre_near, pre_far]
            )
            fc_came = over_y(fc_send)
            proj_total = pair_sum(proj_kept, after(proj_came, fc_send))
            proj_sum = finish(proj_total)
            h1_low = after(h1_low, proj_total)
        else:
            fc_total = pair_sum(fc_kept, after(fc_came, dq))
            fc_sum = finish(fc_total)
            h1_low = after(h1_low, fc_total)
        send_x, keep_x, send_y, keep_y = attention_weights(
            place,
            h1_low,
            h1_other,
            left_b,
            left_b_other,
            [dq, dk, dk_other, dv, dv_other, grad_after_low[:, columns]],
            came,
        )
        terms.append((over_x(send_x), over_y(send_y), keep_x, keep_y))
        held = (keep_x,)
        grads.append((dq, dv, came[1], dk, came[0]))
        if not group[0]:
            out_came = after(out_came, keep_x)
            block_tiles = tiled(block_value_of(after_attn, out_near, out_core, out_came, proj_bias_full))
            block_sent = exchange(block_tiles)
    came = after(terms[0][:2], *held)
    second_0 = second_terms(place, *came, *terms[0][2:])
    grad_input_low, sums_one = on_chip(
        lambda *refs: project_back_kernel(spans, *refs),
        "project_back",
        place,
        [tokens_low, after(grad_after, *held, block_tiles, *second_0), gain_one] + [item for group in grads for item in group],
        pieces,
        [((rows, D), low), ((4, D), f32)],
        [
            pltpu.VMEM((3, D, D), low),
            pltpu.VMEM((rows, D), f32),
            pltpu.SemaphoreType.DMA((3, 2)),
        ],
    )
    came = after((over_y(second_0[0]), over_x(second_0[1])), grad_input_low, block_sent)
    total_0 = summed(*came, *second_0[2:])
    sum_0 = finish(total_0)
    input_sent = exchange(tiled(after(grad_input_low, total_0)))
    came = after(terms[1][:2], total_0, proj_sum, fc_sum)
    second_1 = second_terms(place, *came, *terms[1][2:])
    came = (over_y(second_1[0]), over_x(second_1[1]))
    total_1 = summed(*after(came, sum_0), *second_1[2:])
    sum_1 = finish(total_1)
    input_sent = after(input_sent, total_1)
    proj_quarters = share(after(proj_sum, input_sent))
    block_out = from_sequence(after(block_sent, input_sent))
    fc_quarters = share(after(fc_sum, block_out))
    grad_fc_shard = merge_units(fc_quarters)
    grad_proj_shard = (
        proj_quarters.reshape(2, 2, shard_rows, D)
        .transpose(1, 0, 2, 3)
        .reshape(4 * shard_rows, D)
        .astype(f32)
    )
    share_0 = share(after(sum_0, fc_quarters))
    input_grad = from_sequence(input_sent).astype(f32)
    sum_1 = after(sum_1, input_grad, grad_fc_shard, grad_proj_shard)
    share_1 = share(sum_1)
    quarters = [share_0.astype(f32), share_1.astype(f32)]
    grad_qkv_shard = jnp.concatenate([part[index] for index in range(3) for part in quarters], axis=1)
    grad_out_shard = jnp.concatenate([part[3] for part in quarters], axis=1)

    fc_bias_part = jnp.where(
        jnp.arange(4)[None, :, None] == rep, (sum_near + sum_far).reshape(shards, 1, shard_rows), 0.0
    )
    sums = [
        sums_one[0],
        sums_one[1],
        sums_one[2:],
        sums_two[2],
        sums_two[0],
        sums_two[1],
        fc_bias_part,
        sums_two[3],
    ]
    table = jnp.concatenate([item.reshape(shards, -1) for item in sums], axis=1)
    table = after(table, total_1)
    table = table + over_core(table)
    table = (table + over_x(table)).reshape(2, chips, -1)
    table = lax.dynamic_index_in_dim(table, dp, 0, keepdims=False) + over_y(
        lax.dynamic_index_in_dim(table, 1 - dp, 0, keepdims=False)
    )
    mine = jnp.sum(lax.all_to_all(table[:, None], "ctx", 0, 0, tiled=True), axis=(0, 1))
    small_out, at = [], 0
    for item in sums:
        count = item.size // shards
        small_out.append(mine[at : at + count])
        at += count
    return (
        block_out,
        input_grad,
        small_out[0],
        small_out[1],
        grad_qkv_shard,
        small_out[2],
        grad_out_shard,
        small_out[3],
        small_out[4],
        small_out[5],
        grad_fc_shard,
        small_out[6],
        grad_proj_shard,
        small_out[7],
    )


def local(hidden_in, *rest):
    seqs, block, _ = hidden_in.shape
    sizes = tuple(lax.axis_size(name) for name in ("rep", "dp", "ctx"))
    if sizes[:2] == (4, 2) and 2 * seqs == sizes[2] and sizes[2] * block == SEQ and block == PIECE:
        return sequence_local(hidden_in, *rest)
    return general_local(hidden_in, *rest)


def solution(mesh):
    placed = (
        P(("rep", "dp"), "ctx", None),
        P(("rep", "dp"), None),
        P(("rep", "dp"), "ctx", None),
        P(("dp", "ctx")),
        P(("dp", "ctx")),
        P(("dp", "ctx"), None),
        P(("dp", "ctx")),
        P(("dp", "ctx"), None),
        P(("dp", "ctx")),
        P(("dp", "ctx")),
        P(("dp", "ctx")),
        P(("dp", "ctx"), None),
        P(("dp", "ctx")),
        P(("dp", "ctx"), None),
        P(("dp", "ctx")),
    )
    return jax.shard_map(
        local,
        mesh=mesh,
        in_specs=placed,
        out_specs=(
            P(("rep", "dp"), "ctx", None),
            P(("rep", "dp"), "ctx", None),
            P(("dp", "ctx")),
            P(("dp", "ctx")),
            P(("dp", "ctx"), None),
            P(("dp", "ctx")),
            P(("dp", "ctx"), None),
            P(("dp", "ctx")),
            P(("dp", "ctx")),
            P(("dp", "ctx")),
            P(("dp", "ctx"), None),
            P(("dp", "ctx")),
            P(("dp", "ctx"), None),
            P(("dp", "ctx")),
        ),
        check_vma=False,
    )
```
